256 devices in a mesh: leaf: 16 (over x, y), rows: 16 (over z, core).
Axes of the slice: x: 4, y: 4, z: 8, core: 2. Of those that a mesh axis runs over, the one named last changes fastest.
Arguments:
- rhs_top: float32 [1, 4096, 128], P(None, 'rows'), may hold values from -6 to 6
- rhs_one: float32 [2, 2048, 128], P(None, 'rows'), may hold values from -6 to 6
- rhs_two: float32 [4, 2048, 128], P(None, 'rows'), may hold values from -6 to 6
- rhs_three: float32 [8, 1024, 128], P(None, 'rows'), may hold values from -6 to 6
- inv_top: float32 [4096, 4096], P('rows', 'leaf')
- inv_one: float32 [2048, 4096], P('rows', 'leaf')
- inv_two: float32 [2048, 8192], P('rows', 'leaf')
- inv_three: float32 [1024, 8192], P('rows', 'leaf')
- panel_one: float32 [4096, 2048], P('leaf', 'rows'), may hold values from -0.0625 to 0.0625
- panel_two: float32 [8192, 4096], P('leaf', 'rows'), may hold values from -0.0625 to 0.0625
- panel_three: float32 [8192, 4096], P('leaf', 'rows'), may hold values from -0.09375 to 0.09375
- rows_one: int32 [2, 16], P(None, 'rows'), may hold values from 0 to 31, as said below
- rows_two: int32 [4, 32], P(None, 'rows'), may hold values from 0 to 47, as said below
- rows_three: int32 [8, 32], P(None, 'rows'), may hold values from 0 to 63, as said below
Outputs:
- solution_top: float32 [1, 4096, 128], P(None, 'rows')
- solution_one: float32 [2, 2048, 128], P(None, 'rows')
- solution_two: float32 [4, 2048, 128], P(None, 'rows')
- solution_three: float32 [8, 1024, 128], P(None, 'rows')
The draws below stay inside these ranges and needn't reach their ends.
Inputs may be any that keep to these rules, and one draw needn't show every extreme that they name: `rows_one`: each row lists 16 different blocks of a chain of 32 blocks, the chain's first and last among them. `rows_two`: each row lists 32 different blocks of a chain of 48 blocks, the chain's first and last among them. `rows_three`: each row lists 32 different blocks of a chain of 64 blocks, the chain's first and last among them.
All inputs are finite; a program needn't handle non-finite values.
Results may differ from the reference program's by a relative error of at most 0.0001.
Values sent between devices are 32-bit elements; how exact they have to be, the bound alone decides.
A program may use at most 64 MiB of HBM per device.

```python
import jax
import jax.numpy as jnp
from jax import lax

SEP0 = 4096
SEP1 = 2048
SEP2 = 2048
SEP3 = 1024
BLOCK = 128
K1 = 16
K2 = 32
K3 = 32
NRHS = 128


def dense_inverse(key, sep_size, sep_count):
    first_key, second_key = jax.random.split(key)
    full_shape = (sep_size, sep_count * sep_size)
    column_ids = lax.broadcasted_iota(jnp.int32, full_shape, 0)
    row_ids = lax.broadcasted_iota(jnp.int32, full_shape, 1) % sep_size
    scatter_part = jax.random.normal(first_key, full_shape, jnp.float32) / sep_size ** 0.5
    diagonal = jax.random.uniform(second_key, full_shape, jnp.float32, 0.5, 1.0)
    return scatter_part + jnp.where(row_ids == column_ids, diagonal, 0.0)


def chain_rows(key, sep_count, chain_count, listed):

    def one_row(sep_number):
        order = jax.random.permutation(jax.random.fold_in(key, sep_number), chain_count - 2) + 1
        fixed_ends = jnp.array([chain_count - 1, 0], jnp.int32)
        return jnp.concatenate([fixed_ends, order[:listed - 2].astype(jnp.int32)])
    return jax.vmap(one_row)(jnp.arange(sep_count, dtype=jnp.int32))


def draw_inv_top(key, part):
    return dense_inverse(key, SEP0, 1)


def draw_inv_one(key, part):
    return dense_inverse(key, SEP1, 2)


def draw_inv_two(key, part):
    return dense_inverse(key, SEP2, 4)


def draw_inv_three(key, part):
    return dense_inverse(key, SEP3, 8)


def draw_rows_one(key, part):
    return chain_rows(key, 2, SEP0 // BLOCK, K1)


def draw_rows_two(key, part):
    return chain_rows(key, 4, (SEP0 + SEP1) // BLOCK, K2)


def draw_rows_three(key, part):
    return chain_rows(key, 8, (SEP0 + SEP1 + SEP2) // BLOCK, K3)


def block_levels(own_key, dims, cuts, low, largest):
    def one(dim, shards_of):
        draws = jax.random.uniform(jax.random.fold_in(jax.random.fold_in(own_key, 6), dim), (shards_of,), jnp.float32, low / len(cuts), largest / len(cuts))
        return jnp.repeat(jnp.exp(draws), dims[dim] // shards_of).reshape((-1,) + (1,) * (len(dims) - dim - 1))

    loudness = one(*cuts[0])
    for cut in cuts[1:]:
        loudness = loudness * one(*cut)
    return loudness


def scatter_about(stream_key, dims, deviation, bound, cuts=(), kind=jnp.bfloat16):
    drawn = jax.random.normal(stream_key, dims, jnp.float32) * deviation
    if len(cuts) > 0:
        drawn = block_levels(stream_key, dims, cuts, -0.22, 0.18) * drawn
    return jnp.clip(drawn, min=-bound, max=bound).astype(kind)


def setup_inputs(seed: int = 0) -> dict:
    keys = jax.random.split(jax.random.key(seed), 15)
    return {
        "rhs_top": scatter_about(keys[0], (1, SEP0, NRHS), 1.0, 6.0, ((1, 16),), jnp.float32),
        "rhs_one": scatter_about(keys[1], (2, SEP1, NRHS), 1.0, 6.0, ((1, 16),), jnp.float32),
        "rhs_two": scatter_about(keys[2], (4, SEP2, NRHS), 1.0, 6.0, ((1, 16),), jnp.float32),
        "rhs_three": scatter_about(keys[3], (8, SEP3, NRHS), 1.0, 6.0, ((1, 16),), jnp.float32),
        "inv_top": draw_inv_top(jax.random.fold_in(keys[14], 71), 0),
        "inv_one": draw_inv_one(jax.random.fold_in(keys[14], 71), 0),
        "inv_two": draw_inv_two(jax.random.fold_in(keys[14], 71), 0),
        "inv_three": draw_inv_three(jax.random.fold_in(keys[14], 71), 0),
        "panel_one": scatter_about(keys[8], (2 * SEP1, K1 * BLOCK), (4 * SEP1) ** -0.5, 0.0625, ((0, 16), (1, 16)), jnp.float32),
        "panel_two": scatter_about(keys[9], (4 * SEP2, K2 * BLOCK), (4 * SEP2) ** -0.5, 0.0625, ((0, 16), (1, 16)), jnp.float32),
        "panel_three": scatter_about(keys[10], (8 * SEP3, K3 * BLOCK), (4 * SEP3) ** -0.5, 0.09375, ((0, 16), (1, 16)), jnp.float32),
        "rows_one": draw_rows_one(jax.random.fold_in(keys[14], 71), 0),
        "rows_two": draw_rows_two(jax.random.fold_in(keys[14], 71), 0),
        "rows_three": draw_rows_three(jax.random.fold_in(keys[14], 71), 0),
    }


def solve_blocks(inverse, vector, sep_count, sep_size, backward):
    blocks = inverse.reshape(sep_size, sep_count, sep_size)
    if backward:
        return jnp.einsum('cpr,prn->pcn', blocks, vector, precision=lax.Precision.HIGHEST)
    return jnp.einsum('cpr,pcn->prn', blocks, vector, precision=lax.Precision.HIGHEST)


def reference(rhs_top, rhs_one, rhs_two, rhs_three, inv_top, inv_one, inv_two, inv_three, panel_one, panel_two, panel_three, rows_one, rows_two, rows_three):
    sep_sizes = [SEP0, SEP1, SEP2, SEP3]
    sep_counts = [1, 2, 4, 8]
    right_sides = [rhs_top, rhs_one, rhs_two, rhs_three]
    inverses = [inv_top, inv_one, inv_two, inv_three]
    panels = [None, panel_one, panel_two, panel_three]
    indices = [None, rows_one, rows_two, rows_three]
    width_rhs = rhs_top.shape[2]
    owed_rows = [jnp.zeros(item.shape, jnp.float32) for item in right_sides]
    solved = [None, None, None, None]
    cut_panels = [None, None, None, None]
    all_matches = [None, None, None, None]
    for level_at in (3, 2, 1, 0):
        sep_count = sep_counts[level_at]
        sep_size = sep_sizes[level_at]
        source = right_sides[level_at] - owed_rows[level_at]
        solved[level_at] = solve_blocks(inverses[level_at], source, sep_count, sep_size, False)
        if level_at > 0:
            chain_count = sum(sep_sizes[:level_at]) // BLOCK
            width_blocks = panels[level_at].shape[1] // BLOCK
            panel_cut = panels[level_at].reshape(sep_count, sep_size, width_blocks, BLOCK)
            cut_panels[level_at] = panel_cut
            updates = jnp.einsum('pskb,psn->pkbn', panel_cut, solved[level_at], precision=lax.Precision.HIGHEST)
            matches = (jnp.arange(chain_count, dtype=jnp.int32)[None, :, None] == indices[level_at][:, None, :]).astype(jnp.float32)
            all_matches[level_at] = matches
            spread = jnp.einsum('pck,pkbn->pcbn', matches, updates, precision=lax.Precision.HIGHEST)
            owners = jnp.arange(sep_count, dtype=jnp.int32)
            offset = 0
            for upper in range(level_at):
                blocks_up = sep_sizes[upper] // BLOCK
                segment = spread[:, offset:offset + blocks_up].reshape(sep_count, sep_sizes[upper], width_rhs)
                target = (jnp.arange(sep_counts[upper], dtype=jnp.int32)[None, :] == (owners >> (level_at - upper))[:, None]).astype(jnp.float32)
                owed_rows[upper] = owed_rows[upper] + jnp.einsum('pq,prn->qrn', target, segment, precision=lax.Precision.HIGHEST)
                offset = offset + blocks_up
    results = []
    for level_at in range(4):
        sep_count = sep_counts[level_at]
        sep_size = sep_sizes[level_at]
        residue = solved[level_at]
        if level_at > 0:
            chain_count = sum(sep_sizes[:level_at]) // BLOCK
            owners = jnp.arange(sep_count, dtype=jnp.int32)
            pieces = [results[upper][owners >> (level_at - upper)] for upper in range(level_at)]
            chain_x = jnp.concatenate(pieces, axis=1).reshape(sep_count, chain_count, BLOCK, width_rhs)
            chosen = jnp.einsum('pck,pcbn->pkbn', all_matches[level_at], chain_x, precision=lax.Precision.HIGHEST)
            residue = residue - jnp.einsum('pskb,pkbn->psn', cut_panels[level_at], chosen, precision=lax.Precision.HIGHEST)
        results.append(solve_blocks(inverses[level_at], residue, sep_count, sep_size, True))
    return (results[0], results[1], results[2], results[3])
```

```python
import jax
import jax.numpy as jnp
from jax import lax
from jax.experimental import pallas as pl
from jax.experimental.pallas import tpu as pltpu
from jax.sharding import PartitionSpec as P

F32 = jnp.float32
BF16 = jnp.bfloat16
NR = 16
NL = 16
N = 128
MESH = pl.DeviceIdType.MESH

BUFS = {}
PHASES = []


def _pair(name, m):
    BUFS["c_" + name] = (8, m, N)
    BUFS["d_" + name] = (8, m, N)
    PHASES.append(name + "_c")


def _rows_ar(name, m):
    if m == 32:
        BUFS["a_" + name] = (8, 2, m, N)
        BUFS["b_" + name] = (8, m, N)
        BUFS["y_" + name] = (8, 2, m, N)
        _pair(name + "_rs", m)
        PHASES.append(name + "_ag_c")
    else:
        BUFS["a_" + name] = (NR, m, N)
        BUFS["b_" + name] = (NR, m, N)
        BUFS["y_" + name] = (NR, m, N)
    PHASES.extend([name + "_rs", name + "_ag"])


for _name, _m in (("f3", 32), ("f2", 32), ("f1", 16), ("f0", 16), ("g1", 16), ("g2", 32), ("g3", 32)):
    _rows_ar(_name, _m)
for _name, _g, _h in (("two", 4, 32), ("one", 8, 16), ("top", 16, 16)):
    if _h == 32:
        _pair(_name + "_rs", _h)
    BUFS["n_" + _name] = (8, 2, _h, N) if _h == 32 else (NR, _h, N)
    BUFS["m_" + _name] = (8, _h, N) if _h == 32 else (NR, _h, N)
    BUFS["w_" + _name] = (_g, _h, N)
    PHASES.extend([_name + "_rs", _name + "_ag"])
BUFS.update(
    u3=(2, 8, 16, N),
    u2=(2, 8, 16, N),
    u1=(8, 16, N),
    ru32=(4, 2, 2, 16, N),
    ru31=(8, 2, 16, N),
    ru21=(8, 2, 16, N),
    ru30=(16, 2, 16, N),
    ru20=(16, 2, 16, N),
    ru10=(16, 16, N),
    bins0=(NR, 16, N),
    bins1=(NR, 16, N),
    x0p=(16, 16, N),
    x0l=(16, 16, N),
    x0r=(NR, 16, N),
    x0o=(16, 16, N),
    s10=(2, 16, N),
    s20=(4, 2, 16, N),
    s30=(8, 2, 16, N),
    t10=(16, 16, N),
    t20=(16, 2, 16, N),
    t30=(16, 2, 16, N),
    x1p=(8, 16, N),
    x1l=(8, 16, N),
    x1r=(NR, 16, N),
    x1o=(16, 16, N),
    s21=(2, 2, 16, N),
    s31=(4, 2, 16, N),
    t21=(8, 2, 16, N),
    t31=(8, 2, 16, N),
    x2p=(4, 32, N),
    x2l=(4, 32, N),
    x2r=(8, 2, 32, N),
    x2o=(16, 32, N),
    s32=(2, 2, 32, N),
    t32=(4, 2, 32, N),
    x3p=(2, 32, N),
    x3l=(2, 32, N),
    x3o=(16, 32, N),
)
PHASES.extend(("u32", "u31", "u21", "u30", "u20", "u10", "x0l", "x0r", "x0o", "t10", "t20", "t30"))
PHASES.extend(("x1l", "x1r", "x1o", "t21", "t31", "x2l", "x2r", "x2o", "t32", "x3l", "x3o", "x2r_c"))
BUF_NAMES = list(BUFS)
PHASE_ID = {name: at for at, name in enumerate(PHASES)}
WEIGHTS = (
    ("i0", (256, 256)),
    ("i1", (128, 256)),
    ("i2", (128, 512)),
    ("i3", (64, 512)),
    ("p1", (256, 128)),
    ("p2", (512, 256)),
    ("p3", (512, 256)),
)
RIGHT = ((256, N), (128, N), (128, N), (64, N))


def split(value):
    high = value.astype(BF16)
    return high, (value - high.astype(F32)).astype(BF16)


def kernel(*refs):
    rhs_in = refs[:4]
    weight_in = dict(zip([name for name, _ in WEIGHTS], refs[4:11]))
    r1, r2, r3 = refs[11:14]
    out0, out1, out2, out3 = refs[14:18]
    buf = dict(zip(BUF_NAMES, refs[18 : 18 + len(BUF_NAMES)]))
    at = 18 + len(BUF_NAMES)
    whi = dict(zip([name for name, _ in WEIGHTS], refs[at : at + 7]))
    wlo = dict(zip([name for name, _ in WEIGHTS], refs[at + 7 : at + 14]))
    w32 = dict(zip([name for name, _ in WEIGHTS], refs[at + 14 : at + 21]))
    rhs = refs[at + 21 : at + 25]
    load_sem, send_sem, recv_sem = refs[at + 25 :]

    leaf = lax.axis_index("leaf")
    row = lax.axis_index("rows")
    q1, q2, q3 = lax.div(leaf, 8), lax.div(leaf, 4), lax.div(leaf, 2)
    pos = {16: leaf, 8: lax.rem(leaf, 8), 4: lax.rem(leaf, 4), 2: lax.rem(leaf, 2)}

    loads = {}

    def load(name, src, dst):
        loads[name] = pltpu.make_async_copy(src, dst, load_sem.at[len(loads)])
        loads[name].start()

    load("i3", weight_in["i3"], w32["i3"])
    for at, sep in ((3, q3), (2, q2), (1, q1), (0, 0)):
        load(at, rhs_in[at].at[sep], rhs[at])
    for name in ("p3", "i2", "p2", "i1", "p1", "i0"):
        load(name, weight_in[name], w32[name])

    def ready(*names):
        for name in names:
            loads[name].wait()
            whi[name][...], wlo[name][...] = split(w32[name][...])

    z, core = lax.div(row, 2), lax.rem(row, 2)
    partner = {"rows": row + 1 - 2 * core}

    def z_peer(step):
        half = lax.div(step + 1, 2)
        sign = 1 - 2 * lax.rem(step, 2)
        return lax.rem(z + 4 + half * sign, 8)

    def row_peer(step):
        half = lax.div(step + 1, 2)
        sign = 1 - 2 * lax.rem(step, 2)
        return lax.rem(row + 8 + half * sign, NR)

    barrier = pltpu.get_barrier_semaphore()

    def hello(step, carry):
        pl.semaphore_signal(barrier, inc=1, device_id={"rows": lax.rem(row + 1 + step, NR)}, device_id_type=MESH)
        pl.semaphore_signal(barrier, inc=1, device_id={"leaf": lax.rem(leaf + 1 + step, NL)}, device_id_type=MESH)
        return carry

    lax.fori_loop(0, 15, hello, 0)

    pending = []

    def remote(src, dst, phase, device):
        return pltpu.make_async_remote_copy(
            src_ref=src,
            dst_ref=dst,
            send_sem=send_sem.at[PHASE_ID[phase]],
            recv_sem=recv_sem.at[PHASE_ID[phase]],
            device_id=device,
            device_id_type=MESH,
        )

    def rows_send(phase, src, dst, whole):
        def go(step, carry):
            peer = row_peer(step)
            remote(src(peer), dst, phase, {"rows": peer}).start()
            return carry

        lax.fori_loop(0, NR - 1, go, 0)
        pending.append((phase, whole))

    def leaf_send(phase, group, src, dst, whole):
        base = leaf - pos[group]

        def go(step, carry):
            to = lax.rem(pos[group] + 1 + step, group)
            remote(src(to), dst, phase, {"leaf": base + to}).start()
            return carry

        lax.fori_loop(0, group - 1, go, 0)
        pending.append((phase, whole))

    def arrived(phase, whole):
        remote(whole, whole, phase, {"rows": lax.rem(row + 1, NR)}).wait_recv()

    def mm(name, x, transposed):
        xh, xl = split(x)
        both = jnp.concatenate([xh, xl], axis=1)
        dims = (((0,), (0,)), ((), ())) if transposed else (((1,), (0,)), ((), ()))
        first = lax.dot_general(whi[name][...], both, dims, preferred_element_type=F32)
        second = lax.dot_general(wlo[name][...], xh, dims, preferred_element_type=F32)
        return first[:, :N] + first[:, N:] + second

    def total(ref, count):
        terms = [ref[j] for j in range(count)]
        while len(terms) > 1:
            terms = [a + b for a, b in zip(terms[::2], terms[1::2])]
        return terms[0]

    def z_send(phase, src, dst, whole):
        def go(step, carry):
            peer = z_peer(step)
            remote(src(peer), dst, phase, {"rows": 2 * peer + core}).start()
            return carry

        lax.fori_loop(0, 7, go, 0)
        pending.append((phase, whole))

    def pair_reduce(phase, out, land, fill=None):
        other, both = buf["c_" + phase], buf["d_" + phase]
        remote(out.at[:, 1 - core], other, phase + "_c", partner).start()
        pending.append((phase + "_c", other))
        arrived(phase + "_c", other)
        both[...] = out[:, core] + other[...]
        some = land.at[pl.ds(0, 7)]
        z_send(phase, lambda peer: both.at[peer], land.at[z], some)
        land[z] = both[z]
        if fill is not None:
            fill()
        arrived(phase, some)
        return total(land, 8)

    def pair_gather(phase, piece, full, fill=None):
        full[z, core] = piece
        some = full.at[pl.ds(0, 7), 0]
        z_send(phase, lambda peer: full.at[z, core], full.at[z, core], some)
        if fill is not None:
            fill()
        arrived(phase, some)
        mine = full.at[:, core]
        remote(mine, mine, phase + "_c", partner).start()
        pending.append((phase + "_c", mine))
        arrived(phase + "_c", mine)

    def rows_reduce(phase, out, land, fill=None):
        some = land.at[pl.ds(0, NR - 1)]
        rows_send(phase, lambda peer: out.at[peer], land.at[row], some)
        land[row] = out[row]
        if fill is not None:
            fill()
        arrived(phase, some)
        return total(land, NR)

    def rows_gather(phase, piece, full, fill=None):
        full[row] = piece
        some = full.at[pl.ds(0, NR - 1)]
        rows_send(phase, lambda peer: full.at[row], full.at[row], some)
        if fill is not None:
            fill()
        arrived(phase, some)

    def leaf_gather_start(phase, group, piece, full):
        full[pos[group]] = piece
        some = full.at[pl.ds(0, group - 1)]
        leaf_send(phase, group, lambda to: full.at[pos[group]], full.at[pos[group]], some)
        return some

    def leaf_gather(phase, group, piece, full):
        arrived(phase, leaf_gather_start(phase, group, piece, full))

    def leaf_exchange(phase, group, src, land, own):
        some = land.at[pl.ds(0, group - 1)]
        leaf_send(phase, group, src, land.at[pos[group]], some)
        land[pos[group]] = own
        return some

    def rows_sum(name, value, fill=None, fill2=None):
        out, land, full = buf["a_" + name], buf["b_" + name], buf["y_" + name]
        out[...] = value.reshape(out.shape)
        paired = len(out.shape) == 4
        piece = (pair_reduce if paired else rows_reduce)(name + "_rs", out, land, fill)
        (pair_gather if paired else rows_gather)(name + "_ag", piece, full, fill2)

    def rows_value(name):
        full = buf["y_" + name]
        return full[...].reshape(-1, N)

    ready("i3")
    loads[3].wait()
    first = mm("i3", rhs[3][...], True)
    pl.semaphore_wait(barrier, 30)

    def ready_two():
        ready("i2", "p2")
        loads[2].wait()
        loads[1].wait()
        loads[0].wait()

    rows_sum("f3", first, lambda: ready("p3"), ready_two)
    u3 = buf["u3"]
    u3[...] = mm("p3", rows_value("f3"), True).reshape(u3.shape)
    ru32 = buf["ru32"]
    some = leaf_exchange(
        "u32", 4, lambda to: u3.at[:, pl.ds(2 * to, 2)], ru32, u3[:, pl.ds(2 * pos[4], 2)]
    )
    arrived("u32", some)

    def bins(dst, terms, base, shape, add=None):
        for s in range(NR):
            value = None if add is None else add[s]
            for index, piece in terms:
                one = jnp.where(index == base(s), piece, jnp.zeros(shape, F32))
                value = one if value is None else value + one
            if len(dst.shape) == 4:
                dst[s // 2, s % 2] = value
            else:
                dst[s] = value

    terms = []
    for p in range(2):
        for k in range(2):
            piece = (ru32[2 * p, k] + ru32[2 * p + 1, k]).reshape(32, N)
            terms.append((r3[k, 2 * q2 + p], piece))
    bins(buf["n_two"], terms, lambda s: 48 + s, (32, N))

    ru31, ru30 = buf["ru31"], buf["ru30"]

    def start_u3_upper():
        start_u3_upper.one = leaf_exchange("u31", 8, lambda to: u3.at[:, to], ru31, u3[:, pos[8]])
        start_u3_upper.top = leaf_exchange(
            "u30", 16, lambda to: u3.at[:, lax.rem(to, 8)], ru30, u3[:, pos[8]]
        )
        ready("i1", "p1", "i0")

    piece = pair_reduce("two_rs", buf["n_two"], buf["m_two"], start_u3_upper)
    leaf_gather("two_ag", 4, piece, buf["w_two"])
    source = rhs[2][...] - buf["w_two"][...].reshape(128, N)

    def fill_one():
        arrived("u31", start_u3_upper.one)
        terms = []
        for p in range(4):
            for k in range(2):
                terms.append((r3[k, 4 * q1 + p], ru31[2 * p, k] + ru31[2 * p + 1, k]))
        bins(buf["bins1"], terms, lambda s: 32 + s, (16, N))

    def fill_top():
        arrived("u30", start_u3_upper.top)
        terms = []
        for p in range(8):
            for k in range(2):
                terms.append((r3[k, p], ru30[2 * p, k] + ru30[2 * p + 1, k]))
        bins(buf["bins0"], terms, lambda s: 2 * s + q1, (16, N))

    rows_sum("f2", mm("i2", source, True), fill_one, fill_top)
    u2 = buf["u2"]
    u2[...] = mm("p2", rows_value("f2"), True).reshape(u2.shape)
    ru21, ru20 = buf["ru21"], buf["ru20"]
    some = leaf_exchange("u21", 8, lambda to: u2.at[:, to], ru21, u2[:, pos[8]])
    arrived("u21", some)
    terms = []
    for p in range(2):
        for k in range(2):
            piece = (ru21[4 * p, k] + ru21[4 * p + 1, k]) + (ru21[4 * p + 2, k] + ru21[4 * p + 3, k])
            terms.append((r2[k, 2 * q1 + p], piece))
    bins(buf["n_one"], terms, lambda s: 32 + s, (16, N), buf["bins1"])

    def start_u2_upper():
        start_u2_upper.top = leaf_exchange(
            "u20", 16, lambda to: u2.at[:, lax.rem(to, 8)], ru20, u2[:, pos[8]]
        )

    piece = rows_reduce("one_rs", buf["n_one"], buf["m_one"], start_u2_upper)
    leaf_gather("one_ag", 8, piece, buf["w_one"])
    source = rhs[1][...] - buf["w_one"][...].reshape(128, N)

    def fill_top_two():
        arrived("u20", start_u2_upper.top)
        terms = []
        for p in range(4):
            for k in range(2):
                piece = (ru20[4 * p, k] + ru20[4 * p + 1, k]) + (ru20[4 * p + 2, k] + ru20[4 * p + 3, k])
                terms.append((r2[k, p], piece))
        bins(buf["bins0"], terms, lambda s: 2 * s + q1, (16, N), buf["bins0"])

    rows_sum("f1", mm("i1", source, True), fill_top_two)
    u1 = buf["u1"]
    u1[...] = mm("p1", rows_value("f1"), True).reshape(u1.shape)
    ru10 = buf["ru10"]
    some = leaf_exchange("u10", 16, lambda to: u1.at[lax.rem(to, 8)], ru10, u1[pos[8]])
    arrived("u10", some)
    terms = []
    for p in range(2):
        piece = ru10[8 * p]
        for j in range(1, 8):
            piece = piece + ru10[8 * p + j]
        terms.append((r1[0, p], piece))
    bins(buf["n_top"], terms, lambda s: 2 * s + q1, (16, N), buf["bins0"])
    piece = rows_reduce("top_rs", buf["n_top"], buf["m_top"])
    leaf_gather("top_ag", 16, piece, buf["w_top"])
    source = rhs[0][...] - buf["w_top"][...].reshape(256, N)

    rows_sum("f0", mm("i0", source, True))
    x0p, x0l, x0r = buf["x0p"], buf["x0l"], buf["x0r"]
    x0p[...] = mm("i0", rows_value("f0"), False).reshape(x0p.shape)
    some = leaf_exchange("x0l", 16, lambda to: x0p.at[to], x0l, x0p[leaf])
    arrived("x0l", some)
    piece = total(x0l, 16)
    rows_gather("x0r", piece, x0r)

    def pick_top(index):
        held = x0r[jnp.minimum(lax.div(index, 2), 15)]
        mine = jnp.logical_and(index < 32, lax.rem(index, 2) == q1)
        return jnp.where(mine, held, jnp.zeros((16, N), F32))

    s10, t10 = buf["s10"], buf["t10"]
    for p in range(2):
        s10[p] = pick_top(r1[0, p])
    some = leaf_exchange("t10", 16, lambda to: s10.at[lax.div(to, 8)], t10, s10[q1])
    wait_x0o = leaf_gather_start("x0o", 16, piece, buf["x0o"])
    arrived("t10", some)
    chosen = (t10[pl.ds(0, 8)] + t10[pl.ds(8, 8)]).reshape(128, N)

    s20, t20, s30, t30 = buf["s20"], buf["t20"], buf["s30"], buf["t30"]

    def fill_t():
        for p in range(4):
            for k in range(2):
                s20[p, k] = pick_top(r2[k, p])
        fill_t.two = leaf_exchange("t20", 16, lambda to: s20.at[lax.div(to, 4)], t20, s20[q2])
        for p in range(8):
            for k in range(2):
                s30[p, k] = pick_top(r3[k, p])
        fill_t.three = leaf_exchange("t30", 16, lambda to: s30.at[lax.div(to, 2)], t30, s30[q3])

    rows_sum("g1", mm("p1", chosen, False), fill_t)
    x1p, x1l, x1r = buf["x1p"], buf["x1l"], buf["x1r"]
    x1p[...] = mm("i1", rows_value("f1") - rows_value("g1"), False).reshape(x1p.shape)
    some = leaf_exchange("x1l", 8, lambda to: x1p.at[to], x1l, x1p[pos[8]])
    arrived("x1l", some)
    piece = total(x1l, 8)
    rows_gather("x1r", piece, x1r)

    def pick_one(index):
        held = x1r[jnp.clip(index - 32, 0, 15)]
        mine = jnp.logical_and(index >= 32, index < 48)
        return jnp.where(mine, held, jnp.zeros((16, N), F32))

    s21, t21, s31, t31 = buf["s21"], buf["t21"], buf["s31"], buf["t31"]
    for p in range(2):
        for k in range(2):
            s21[p, k] = pick_one(r2[k, 2 * q1 + p])
    some = leaf_exchange("t21", 8, lambda to: s21.at[lax.div(to, 4)], t21, s21[q2 - 2 * q1])
    wait_x1o = leaf_gather_start("x1o", 16, piece, buf["x1o"])
    arrived("t20", fill_t.two)
    arrived("t21", some)
    parts = []
    for k in range(2):
        parts.append(
            (t20[pl.ds(0, 8), k] + t20[pl.ds(8, 8), k] + t21[pl.ds(0, 8), k]).reshape(128, N)
        )

    def fill_o():
        for p in range(4):
            for k in range(2):
                s31[p, k] = pick_one(r3[k, 4 * q1 + p])
        fill_o.three = leaf_exchange(
            "t31", 8, lambda to: s31.at[lax.div(to, 2)], t31, s31[q3 - 4 * q1]
        )

    rows_sum("g2", mm("p2", jnp.concatenate(parts, axis=0), False), fill_o)
    x2p, x2l, x2r = buf["x2p"], buf["x2l"], buf["x2r"]
    x2p[...] = mm("i2", rows_value("f2") - rows_value("g2"), False).reshape(x2p.shape)
    some = leaf_exchange("x2l", 4, lambda to: x2p.at[to], x2l, x2p[pos[4]])
    arrived("x2l", some)
    piece = total(x2l, 4)
    pair_gather("x2r", piece, x2r)

    def pick_two(index):
        at = jnp.clip(index - 48, 0, 15)
        held = x2r[lax.div(at, 2), lax.rem(at, 2)]
        return jnp.where(index >= 48, held, jnp.zeros((32, N), F32))

    s32, t32 = buf["s32"], buf["t32"]
    for p in range(2):
        for k in range(2):
            s32[p, k] = pick_two(r3[k, 2 * q2 + p])
    some = leaf_exchange("t32", 4, lambda to: s32.at[lax.div(to, 2)], t32, s32[q3 - 2 * q2])
    wait_x2o = leaf_gather_start("x2o", 16, piece, buf["x2o"])
    arrived("t30", fill_t.three)
    arrived("t31", fill_o.three)
    arrived("t32", some)
    parts = []
    for k in range(2):
        upper = t30[pl.ds(0, 8), k] + t30[pl.ds(8, 8), k] + t31[pl.ds(0, 8), k]
        parts.append(upper.reshape(128, N) + t32[pl.ds(0, 4), k].reshape(128, N))

    def outputs():
        arrived("x0o", wait_x0o)
        out0[...] = buf["x0o"][...].reshape(out0.shape)
        arrived("x1o", wait_x1o)
        out1[...] = buf["x1o"][...].reshape(out1.shape)
        arrived("x2o", wait_x2o)
        out2[...] = buf["x2o"][...].reshape(out2.shape)

    rows_sum("g3", mm("p3", jnp.concatenate(parts, axis=0), False), outputs)
    x3p, x3l = buf["x3p"], buf["x3l"]
    x3p[...] = mm("i3", rows_value("f3") - rows_value("g3"), False).reshape(x3p.shape)
    some = leaf_exchange("x3l", 2, lambda to: x3p.at[to], x3l, x3p[pos[2]])
    arrived("x3l", some)
    leaf_gather("x3o", 16, total(x3l, 2), buf["x3o"])
    out3[...] = buf["x3o"][...].reshape(out3.shape)

    for phase, whole in pending:
        remote(whole, whole, phase, {"rows": lax.rem(row + 1, NR)}).wait_send()


def store(*refs):
    copies = [pltpu.make_async_copy(refs[j], refs[4 + j], refs[8].at[j]) for j in range(4)]
    for copy in copies:
        copy.start()
    for copy in copies:
        copy.wait()


def body(*args):
    vmem = pl.BlockSpec(memory_space=pltpu.VMEM)
    smem = pl.BlockSpec(memory_space=pltpu.SMEM)
    outs = tuple(jax.ShapeDtypeStruct(item.shape, F32) for item in args[:4])
    solved = tuple(
        pl.pallas_call(
            kernel,
            out_shape=outs,
            in_specs=[pl.BlockSpec(memory_space=pltpu.MemorySpace.HBM)] * 11 + [smem] * 3,
            out_specs=[vmem] * 4,
            scratch_shapes=[pltpu.VMEM(BUFS[name], F32) for name in BUF_NAMES]
            + [pltpu.VMEM(shape, BF16) for _, shape in WEIGHTS] * 2
            + [pltpu.VMEM(shape, F32) for _, shape in WEIGHTS]
            + [pltpu.VMEM(shape, F32) for shape in RIGHT]
            + [pltpu.SemaphoreType.DMA((11,))]
            + [pltpu.SemaphoreType.DMA((len(PHASES),)), pltpu.SemaphoreType.DMA((len(PHASES),))],
            compiler_params=pltpu.CompilerParams(
                collective_id=0, has_side_effects=True, vmem_limit_bytes=60 * 1024 * 1024
            ),
        )(*args[:11], *(item.T for item in args[11:]))
    )
    return tuple(
        pl.pallas_call(
            store,
            out_shape=outs,
            in_specs=[vmem] * 4,
            out_specs=[pl.BlockSpec(memory_space=pltpu.MemorySpace.HBM)] * 4,
            scratch_shapes=[pltpu.SemaphoreType.DMA((4,))],
        )(*solved)
    )


def solution(mesh):
    rhs = P(None, "rows", None)
    return jax.shard_map(
        body,
        mesh=mesh,
        in_specs=(rhs,) * 4
        + (P("rows", "leaf"),) * 4
        + (P("leaf", "rows"),) * 3
        + (P(None, "rows"),) * 3,
        out_specs=(rhs,) * 4,
        check_vma=False,
    )
```

```python
import jax
import jax.numpy as jnp
from jax import lax
from jax.experimental import pallas as pl
from jax.experimental.pallas import tpu as pltpu
from jax.sharding import PartitionSpec as P

F32 = jnp.float32
BF16 = jnp.bfloat16
NR = 16
NL = 16
N = 128
MESH = pl.DeviceIdType.MESH

BUFS = {}
PHASES = []


def _pair(name, m):
    BUFS["c_" + name] = (8, m, N)
    BUFS["d_" + name] = (8, m, N)
    PHASES.append(name + "_c")


def _rows_ar(name, m):
    if m == 32:
        BUFS["a_" + name] = (8, 2, m, N)
        BUFS["b_" + name] = (8, m, N)
        BUFS["y_" + name] = (8, 2, m, N)
        _pair(name + "_rs", m)
        PHASES.append(name + "_ag_c")
    else:
        BUFS["a_" + name] = (NR, m, N)
        BUFS["b_" + name] = (NR, m, N)
        BUFS["y_" + name] = (NR, m, N)
    PHASES.extend([name + "_rs", name + "_ag"])


for _name, _m in (("f3", 32), ("f2", 32), ("f1", 16), ("f0", 16), ("g2", 32), ("g3", 32)):
    _rows_ar(_name, _m)
for _name, _g, _h in (("two", 4, 32), ("one", 8, 16), ("top", 16, 16)):
    if _h == 32:
        _pair(_name + "_rs", _h)
    BUFS["n_" + _name] = (8, 2, _h, N) if _h == 32 else (NR, _h, N)
    BUFS["m_" + _name] = (8, _h, N) if _h == 32 else (NR, _h, N)
    BUFS["w_" + _name] = (16 if _g == 8 else _g, _h, N)
    PHASES.extend([_name + "_rs", _name + "_ag"])
BUFS.update(
    u3=(2, 8, 16, N),
    u2=(2, 8, 16, N),
    ru32=(4, 2, 2, 16, N),
    ru31=(8, 2, 16, N),
    ru21=(8, 2, 16, N),
    ru30=(16, 2, 16, N),
    ru20=(16, 2, 16, N),
    bins0=(NR, 16, N),
    bins1=(NR, 16, N),
    pg=(8, 256, N),
    ph=(8, 256, N),
    wp0=(8, 16, 8, N),
    wp1=(8, 16, 8, N),
    ws0=(16, 8, 8, N),
    ws1=(16, 8, 8, N),
    nt=(NR, 2, 8, N),
    mt=(NR, 2, 8, N),
    wt=(16, 2, 8, N),
    x0p=(2, 16, 8, N),
    x0l=(16, 2, 8, N),
    x0r=(NR, 2, 8, N),
    x0o=(16, 2, 8, N),
    s20=(4, 2, 8, N),
    s30=(8, 2, 8, N),
    t20=(16, 2, 8, N),
    t30=(16, 2, 8, N),
    x1p=(2, 8, 16, N),
    x1l=(16, 16, N),
    x1r=(NR, 16, N),
    x1o=(16, 16, N),
    s21=(2, 2, 16, N),
    s31=(4, 2, 16, N),
    t21=(8, 2, 16, N),
    t31=(8, 2, 16, N),
    x2p=(4, 32, N),
    x2l=(4, 32, N),
    x2r=(8, 2, 32, N),
    x2o=(16, 32, N),
    s32=(2, 2, 32, N),
    t32=(4, 2, 32, N),
    x3p=(2, 32, N),
    x3l=(2, 32, N),
    x3o=(16, 32, N),
)
PHASES.extend(("u32", "u31", "u21", "u30", "u20", "x0l", "x0r", "x0o", "t20", "t30", "tag", "nt", "wt"))
PHASES.extend(("up1", "up2", "up3", "up4", "dn1", "dn2", "dn3", "pc", "ws0", "ws1"))
PHASES.extend(("x1l", "x1r", "x1o", "t21", "t31", "x2l", "x2r", "x2o", "t32", "x3l", "x3o", "x2r_c"))
BUF_NAMES = list(BUFS)
PHASE_ID = {name: at for at, name in enumerate(PHASES)}
WEIGHTS = (
    ("i0", (256, 256)),
    ("i1", (128, 256)),
    ("i2", (128, 512)),
    ("i3", (64, 512)),
    ("p1", (256, 128)),
    ("p2", (512, 256)),
    ("p3", (512, 256)),
)
RIGHT = ((256, N), (2, 128, N), (128, N), (64, N))


def split(value):
    high = value.astype(BF16)
    return high, (value - high.astype(F32)).astype(BF16)


def kernel(*refs):
    rhs_in = refs[:4]
    weight_in = dict(zip([name for name, _ in WEIGHTS], refs[4:11]))
    r1, r2, r3 = refs[11:14]
    out0, out1, out2, out3 = refs[14:18]
    buf = dict(zip(BUF_NAMES, refs[18 : 18 + len(BUF_NAMES)]))
    at = 18 + len(BUF_NAMES)
    whi = dict(zip([name for name, _ in WEIGHTS], refs[at : at + 7]))
    wlo = dict(zip([name for name, _ in WEIGHTS], refs[at + 7 : at + 14]))
    w32 = dict(zip([name for name, _ in WEIGHTS], refs[at + 14 : at + 21]))
    rhs = refs[at + 21 : at + 25]
    w1hi, w1lo, tag, tag_s, load_sem, tag_sem, send_sem, recv_sem = refs[at + 25 :]

    leaf = lax.axis_index("leaf")
    row = lax.axis_index("rows")
    q1, q2, q3 = lax.div(leaf, 8), lax.div(leaf, 4), lax.div(leaf, 2)
    pos = {16: leaf, 8: lax.rem(leaf, 8), 4: lax.rem(leaf, 4), 2: lax.rem(leaf, 2)}

    loads = {}

    def load(name, src, dst):
        loads[name] = pltpu.make_async_copy(src, dst, load_sem.at[len(loads)])
        loads[name].start()

    load("i3", weight_in["i3"], w32["i3"])
    for at, sep in ((3, q3), (2, q2), (0, 0)):
        load(at, rhs_in[at].at[sep], rhs[at])
    load(1, rhs_in[1], rhs[1])
    for name in ("p1", "p3", "i2", "p2", "i1", "i0"):
        load(name, weight_in[name], w32[name])

    def ready(*names):
        for name in names:
            loads[name].wait()
            whi[name][...], wlo[name][...] = split(w32[name][...])

    z, core = lax.div(row, 2), lax.rem(row, 2)
    partner = {"rows": row + 1 - 2 * core}

    def z_peer(step):
        half = lax.div(step + 1, 2)
        sign = 1 - 2 * lax.rem(step, 2)
        return lax.rem(z + 4 + half * sign, 8)

    def row_peer(step):
        half = lax.div(step + 1, 2)
        sign = 1 - 2 * lax.rem(step, 2)
        return lax.rem(row + 8 + half * sign, NR)

    barrier = pltpu.get_barrier_semaphore()

    def hello(step, carry):
        pl.semaphore_signal(barrier, inc=1, device_id={"rows": lax.rem(row + 1 + step, NR)}, device_id_type=MESH)
        pl.semaphore_signal(barrier, inc=1, device_id={"leaf": lax.rem(leaf + 1 + step, NL)}, device_id_type=MESH)
        return carry

    lax.fori_loop(0, 15, hello, 0)

    pending = []

    def remote(src, dst, phase, device):
        return pltpu.make_async_remote_copy(
            src_ref=src,
            dst_ref=dst,
            send_sem=send_sem.at[PHASE_ID[phase]],
            recv_sem=recv_sem.at[PHASE_ID[phase]],
            device_id=device,
            device_id_type=MESH,
        )

    def rows_send(phase, src, dst, whole):
        def go(step, carry):
            peer = row_peer(step)
            remote(src(peer), dst, phase, {"rows": peer}).start()
            return carry

        lax.fori_loop(0, NR - 1, go, 0)
        pending.append((phase, whole))

    def leaf_send(phase, group, src, dst, whole):
        base = leaf - pos[group]

        def go(step, carry):
            to = lax.rem(pos[group] + 1 + step, group)
            remote(src(to), dst, phase, {"leaf": base + to}).start()
            return carry

        lax.fori_loop(0, group - 1, go, 0)
        pending.append((phase, whole))

    def arrived(phase, whole):
        remote(whole, whole, phase, {"rows": lax.rem(row + 1, NR)}).wait_recv()

    def product(high, low, x, transposed):
        xh, xl = split(x)
        both = jnp.concatenate([xh, xl], axis=1)
        dims = (((0,), (0,)), ((), ())) if transposed else (((1,), (0,)), ((), ()))
        first = lax.dot_general(high, both, dims, preferred_element_type=F32)
        second = lax.dot_general(low, xh, dims, preferred_element_type=F32)
        return first[:, :N] + first[:, N:] + second

    def mm(name, x, transposed):
        return product(whi[name][...], wlo[name][...], x, transposed)

    pg, ph = buf["pg"], buf["ph"]
    z_up, z_down = lax.rem(z + 1, 8), lax.rem(z + 7, 8)

    def relay(step):
        if step > 1:
            arrived("up%d" % (step - 1), pg.at[0])
            arrived("dn%d" % (step - 1), pg.at[0])
        up = w32["p1"] if step == 1 else pg.at[lax.rem(z + 9 - step, 8)]
        down = w32["p1"] if step == 1 else pg.at[lax.rem(z + step - 1, 8)]
        mark = "up%d" % step
        remote(up, pg.at[lax.rem(z + 9 - step, 8)], mark, {"rows": 2 * z_up + core}).start()
        pending.append((mark, pg.at[0]))
        if step < 4:
            mark = "dn%d" % step
            remote(down, pg.at[lax.rem(z + step - 1, 8)], mark, {"rows": 2 * z_down + core}).start()
            pending.append((mark, pg.at[0]))

    def relay_end():
        arrived("up4", pg.at[0])
        pg[z] = w32["p1"][...]
        remote(pg, ph, "pc", partner).start()
        pending.append(("pc", pg))

    def composite(source, out, phase):
        def one(at, carry):
            part = product(whi["i1"][...], wlo["i1"][...], source[at], False)
            out[at] = part.T.reshape(16, 8, N)
            return carry

        lax.fori_loop(0, 8, one, 0)
        return leaf_exchange(phase, 16, lambda to: out.at[:, to], buf[phase], out[:, leaf])

    def total(ref, count):
        terms = [ref[j] for j in range(count)]
        while len(terms) > 1:
            terms = [a + b for a, b in zip(terms[::2], terms[1::2])]
        return terms[0]

    def z_send(phase, src, dst, whole):
        def go(step, carry):
            peer = z_peer(step)
            remote(src(peer), dst, phase, {"rows": 2 * peer + core}).start()
            return carry

        lax.fori_loop(0, 7, go, 0)
        pending.append((phase, whole))

    def pair_reduce(phase, out, land, fill=None):
        other, both = buf["c_" + phase], buf["d_" + phase]
        remote(out.at[:, 1 - core], other, phase + "_c", partner).start()
        pending.append((phase + "_c", other))
        arrived(phase + "_c", other)
        both[...] = out[:, core] + other[...]
        some = land.at[pl.ds(0, 7)]
        z_send(phase, lambda peer: both.at[peer], land.at[z], some)
        land[z] = both[z]
        if fill is not None:
            fill()
        arrived(phase, some)
        return total(land, 8)

    def pair_gather(phase, piece, full, fill=None):
        full[z, core] = piece
        some = full.at[pl.ds(0, 7), 0]
        z_send(phase, lambda peer: full.at[z, core], full.at[z, core], some)
        if fill is not None:
            fill()
        arrived(phase, some)
        mine = full.at[:, core]
        remote(mine, mine, phase + "_c", partner).start()
        pending.append((phase + "_c", mine))
        arrived(phase + "_c", mine)

    def rows_reduce(phase, out, land, fill=None):
        some = land.at[pl.ds(0, NR - 1)]
        rows_send(phase, lambda peer: out.at[peer], land.at[row], some)
        land[row] = out[row]
        if fill is not None:
            fill()
        arrived(phase, some)
        return total(land, NR)

    def rows_gather(phase, piece, full, fill=None):
        full[row] = piece
        some = full.at[pl.ds(0, NR - 1)]
        rows_send(phase, lambda peer: full.at[row], full.at[row], some)
        if fill is not None:
            fill()
        arrived(phase, some)

    def leaf_gather_start(phase, group, piece, full):
        full[pos[group]] = piece
        some = full.at[pl.ds(0, group - 1)]
        leaf_send(phase, group, lambda to: full.at[pos[group]], full.at[pos[group]], some)
        return some

    def leaf_gather(phase, group, piece, full):
        arrived(phase, leaf_gather_start(phase, group, piece, full))

    def leaf_exchange(phase, group, src, land, own):
        some = land.at[pl.ds(0, group - 1)]
        leaf_send(phase, group, src, land.at[pos[group]], some)
        land[pos[group]] = own
        return some

    def rows_sum(name, value, fill=None, fill2=None):
        out, land, full = buf["a_" + name], buf["b_" + name], buf["y_" + name]
        out[...] = value.reshape(out.shape)
        paired = len(out.shape) == 4
        piece = (pair_reduce if paired else rows_reduce)(name + "_rs", out, land, fill)
        (pair_gather if paired else rows_gather)(name + "_ag", piece, full, fill2)

    def rows_value(name):
        full = buf["y_" + name]
        return full[...].reshape(-1, N)

    ready("i3")
    loads[3].wait()
    first = mm("i3", rhs[3][...], True)
    pl.semaphore_wait(barrier, 30)

    def ready_two():
        ready("i2", "p2")
        loads[2].wait()
        loads[1].wait()
        loads[0].wait()

    def send_tags():
        here = lax.broadcasted_iota(jnp.int32, (8, N), 0)
        tag[row] = jnp.where(here == 0, r1[0, 0], r1[0, 1])
        send_tags.some = tag.at[pl.ds(0, NR - 1)]
        rows_send("tag", lambda peer: tag.at[row], tag.at[row], send_tags.some)

    def slot_one():
        loads["p1"].wait()
        relay(1)
        send_tags()
        ready("p3")

    def slot_two():
        relay(2)
        ready_two()

    rows_sum("f3", first, slot_one, slot_two)
    u3 = buf["u3"]
    u3[...] = mm("p3", rows_value("f3"), True).reshape(u3.shape)
    ru32 = buf["ru32"]
    some = leaf_exchange(
        "u32", 4, lambda to: u3.at[:, pl.ds(2 * to, 2)], ru32, u3[:, pl.ds(2 * pos[4], 2)]
    )
    relay(3)
    arrived("u32", some)

    def bins(dst, terms, base, shape, add=None):
        for s in range(NR):
            value = None if add is None else add[s]
            for index, piece in terms:
                one = jnp.where(index == base(s), piece, jnp.zeros(shape, F32))
                value = one if value is None else value + one
            if len(dst.shape) == 4:
                dst[s // 2, s % 2] = value
            else:
                dst[s] = value

    terms = []
    for p in range(2):
        for k in range(2):
            piece = (ru32[2 * p, k] + ru32[2 * p + 1, k]).reshape(32, N)
            terms.append((r3[k, 2 * q2 + p], piece))
    bins(buf["n_two"], terms, lambda s: 48 + s, (32, N))

    ru31, ru30 = buf["ru31"], buf["ru30"]

    def start_u3_upper():
        start_u3_upper.one = leaf_exchange("u31", 8, lambda to: u3.at[:, to], ru31, u3[:, pos[8]])
        start_u3_upper.top = leaf_exchange(
            "u30", 16, lambda to: u3.at[:, lax.rem(to, 8)], ru30, u3[:, pos[8]]
        )
        relay(4)
        ready("i1", "i0")

    piece = pair_reduce("two_rs", buf["n_two"], buf["m_two"], start_u3_upper)
    some = leaf_gather_start("two_ag", 4, piece, buf["w_two"])
    relay_end()
    arrived("two_ag", some)
    source = rhs[2][...] - buf["w_two"][...].reshape(128, N)

    def fill_one():
        arrived("u31", start_u3_upper.one)
        terms = []
        for p in range(4):
            for k in range(2):
                terms.append((r3[k, 4 * q1 + p], ru31[2 * p, k] + ru31[2 * p + 1, k]))
        bins(buf["bins1"], terms, lambda s: 32 + s, (16, N))

    def fill_top():
        arrived("u30", start_u3_upper.top)
        terms = []
        for p in range(8):
            for k in range(2):
                terms.append((r3[k, p], ru30[2 * p, k] + ru30[2 * p + 1, k]))
        bins(buf["bins0"], terms, lambda s: 2 * s + q1, (16, N))

    def slot_three():
        slot_three.some = composite(pg, buf["wp0"], "ws0")

    def slot_four():
        arrived("pc", ph)
        slot_four.some = composite(ph, buf["wp1"], "ws1")

    rows_sum("f2", mm("i2", source, True), slot_three, slot_four)
    u2 = buf["u2"]
    u2[...] = mm("p2", rows_value("f2"), True).reshape(u2.shape)
    ru21, ru20 = buf["ru21"], buf["ru20"]
    some = leaf_exchange("u21", 8, lambda to: u2.at[:, to], ru21, u2[:, pos[8]])
    some_top = leaf_exchange("u20", 16, lambda to: u2.at[:, lax.rem(to, 8)], ru20, u2[:, pos[8]])
    fill_one()
    arrived("u21", some)
    terms = []
    for p in range(2):
        for k in range(2):
            piece = (ru21[4 * p, k] + ru21[4 * p + 1, k]) + (ru21[4 * p + 2, k] + ru21[4 * p + 3, k])
            terms.append((r2[k, 2 * q1 + p], piece))
    bins(buf["n_one"], terms, lambda s: 32 + s, (16, N), buf["bins1"])

    def fill_top_two():
        fill_top()
        arrived("u20", some_top)
        terms = []
        for p in range(4):
            for k in range(2):
                piece = (ru20[4 * p, k] + ru20[4 * p + 1, k]) + (ru20[4 * p + 2, k] + ru20[4 * p + 3, k])
                terms.append((r2[k, p], piece))
        bins(buf["n_top"], terms, lambda s: 2 * s + q1, (16, N), buf["bins0"])
        ws0, ws1 = buf["ws0"], buf["ws1"]
        arrived("ws0", slot_three.some)
        arrived("ws1", slot_four.some)
        for p in range(2):
            halves = []
            for ws in (ws0, ws1):
                half = ws[8 * p]
                for j in range(1, 8):
                    half = half + ws[8 * p + j]
                halves.append(half.reshape(64, N))
            high, low = split(jnp.concatenate(halves, axis=0))
            w1hi[p] = high
            w1lo[p] = low
        arrived("tag", send_tags.some)
        copy = pltpu.make_async_copy(tag, tag_s, tag_sem)
        copy.start()
        copy.wait()

    piece = rows_reduce("one_rs", buf["n_one"], buf["m_one"], fill_top_two)
    n_top, m_top = buf["n_top"], buf["m_top"]
    some_one = leaf_gather_start("one_ag", 16, piece, buf["w_one"])
    some_top = m_top.at[pl.ds(0, NR - 1)]
    rows_send("top_rs", lambda peer: n_top.at[peer], m_top.at[row], some_top)
    m_top[row] = n_top[row]
    arrived("one_ag", some_one)
    source = [rhs[1][p] - buf["w_one"][pl.ds(8 * p, 8)].reshape(128, N) for p in range(2)]

    def listed(p, k):
        return tag_s[k, p, 0]

    def block_at(j):
        return 2 * lax.rem(jnp.int32(j), 8) + (core if j < 8 else 1 - core)

    indices = [[listed(p, block_at(j)) for j in range(16)] for p in range(2)]
    terms = []
    for p in range(2):
        update = product(w1hi[p], w1lo[p], source[p], False)
        terms.extend((indices[p][j], update[8 * j : 8 * j + 8]) for j in range(16))
    nt = buf["nt"]
    for s in range(NR):
        for half in range(2):
            value = None
            for index, piece in terms:
                one = jnp.where(index == 2 * s + half, piece, jnp.zeros((8, N), F32))
                value = one if value is None else value + one
            nt[s, half] = value

    f1a, f1b = buf["a_f1"], buf["b_f1"]
    some_f1 = f1b.at[pl.ds(0, NR - 1)]

    def start_y1():
        arrived("top_rs", some_top)
        start_y1.top = leaf_gather_start("top_ag", 16, total(m_top, NR), buf["w_top"])
        mine = jnp.where(q1 == 0, source[0], source[1])
        f1a[...] = mm("i1", mine, True).reshape(f1a.shape)
        rows_send("f1_rs", lambda peer: f1a.at[peer], f1b.at[row], some_f1)
        f1b[row] = f1a[row]

    piece = rows_reduce("nt", nt, buf["mt"], start_y1)
    wt = buf["wt"]
    some = leaf_gather_start("wt", 16, piece, wt)
    arrived("top_ag", start_y1.top)
    arrived("wt", some)
    owed = jnp.concatenate([wt[:, 0].reshape(128, N), wt[:, 1].reshape(128, N)], axis=0)
    source = rhs[0][...] - (buf["w_top"][...].reshape(256, N) + owed)

    f1y = buf["y_f1"]

    def gather_y1():
        arrived("f1_rs", some_f1)
        f1y[row] = total(f1b, NR)
        gather_y1.some = f1y.at[pl.ds(0, NR - 1)]
        rows_send("f1_ag", lambda peer: f1y.at[row], f1y.at[row], gather_y1.some)

    def solve_y1():
        arrived("f1_ag", gather_y1.some)
        solve_y1.value = mm("i1", rows_value("f1"), False)

    rows_sum("f0", mm("i0", source, True), gather_y1, solve_y1)
    x0p, x0l, x0r = buf["x0p"], buf["x0l"], buf["x0r"]
    x0p[...] = mm("i0", rows_value("f0"), False).reshape(x0p.shape)
    some = leaf_exchange("x0l", 16, lambda to: x0p.at[:, to], x0l, x0p[:, leaf])
    arrived("x0l", some)
    piece = total(x0l, 16)
    rows_gather("x0r", piece, x0r)

    def pick_top(index):
        at = jnp.minimum(index, 31)
        held = x0r[lax.div(at, 2), lax.rem(at, 2)]
        return jnp.where(index < 32, held, jnp.zeros((8, N), F32))

    x1p = buf["x1p"]
    for p in range(2):
        chosen = jnp.concatenate([pick_top(indices[p][j]) for j in range(16)], axis=0)
        x1p[p] = -product(w1hi[p], w1lo[p], chosen, True).reshape(8, 16, N)
    x1p[q1] = x1p[q1] + solve_y1.value.reshape(8, 16, N)
    x1l, x1r = buf["x1l"], buf["x1r"]
    some = leaf_exchange("x1l", 16, lambda to: x1p.at[lax.div(to, 8), lax.rem(to, 8)], x1l, x1p[q1, pos[8]])
    wait_x0o = leaf_gather_start("x0o", 16, piece, buf["x0o"])

    s20, t20, s30, t30 = buf["s20"], buf["t20"], buf["s30"], buf["t30"]
    for p in range(4):
        for k in range(2):
            s20[p, k] = pick_top(r2[k, p])
    for p in range(8):
        for k in range(2):
            s30[p, k] = pick_top(r3[k, p])
    arrived("x1l", some)
    piece = total(x1l, 16)

    def fill_t():
        fill_t.two = leaf_exchange("t20", 16, lambda to: s20.at[lax.div(to, 4)], t20, s20[q2])
        fill_t.three = leaf_exchange("t30", 16, lambda to: s30.at[lax.div(to, 2)], t30, s30[q3])

    rows_gather("x1r", piece, x1r, fill_t)

    def pick_one(index):
        held = x1r[jnp.clip(index - 32, 0, 15)]
        mine = jnp.logical_and(index >= 32, index < 48)
        return jnp.where(mine, held, jnp.zeros((16, N), F32))

    s21, t21, s31, t31 = buf["s21"], buf["t21"], buf["s31"], buf["t31"]
    for p in range(2):
        for k in range(2):
            s21[p, k] = pick_one(r2[k, 2 * q1 + p])
    some = leaf_exchange("t21", 8, lambda to: s21.at[lax.div(to, 4)], t21, s21[q2 - 2 * q1])
    wait_x1o = leaf_gather_start("x1o", 16, piece, buf["x1o"])
    arrived("t20", fill_t.two)
    arrived("t21", some)
    parts = []
    for k in range(2):
        parts.append(
            t20[:, k].reshape(128, N) + t21[:, k].reshape(128, N)
        )

    def fill_o():
        for p in range(4):
            for k in range(2):
                s31[p, k] = pick_one(r3[k, 4 * q1 + p])
        fill_o.three = leaf_exchange(
            "t31", 8, lambda to: s31.at[lax.div(to, 2)], t31, s31[q3 - 4 * q1]
        )

    rows_sum("g2", mm("p2", jnp.concatenate(parts, axis=0), False), fill_o)
    x2p, x2l, x2r = buf["x2p"], buf["x2l"], buf["x2r"]
    x2p[...] = mm("i2", rows_value("f2") - rows_value("g2"), False).reshape(x2p.shape)
    some = leaf_exchange("x2l", 4, lambda to: x2p.at[to], x2l, x2p[pos[4]])
    arrived("x2l", some)
    piece = total(x2l, 4)
    pair_gather("x2r", piece, x2r)

    def pick_two(index):
        at = jnp.clip(index - 48, 0, 15)
        held = x2r[lax.div(at, 2), lax.rem(at, 2)]
        return jnp.where(index >= 48, held, jnp.zeros((32, N), F32))

    s32, t32 = buf["s32"], buf["t32"]
    for p in range(2):
        for k in range(2):
            s32[p, k] = pick_two(r3[k, 2 * q2 + p])
    some = leaf_exchange("t32", 4, lambda to: s32.at[lax.div(to, 2)], t32, s32[q3 - 2 * q2])
    wait_x2o = leaf_gather_start("x2o", 16, piece, buf["x2o"])
    arrived("t30", fill_t.three)
    arrived("t31", fill_o.three)
    arrived("t32", some)
    parts = []
    for k in range(2):
        upper = t30[:, k].reshape(128, N) + t31[:, k].reshape(128, N)
        parts.append(upper + t32[:, k].reshape(128, N))

    def outputs():
        arrived("x0o", wait_x0o)
        for half in range(2):
            out0[0, pl.ds(128 * half, 128)] = buf["x0o"][:, half].reshape(128, N)
        arrived("x1o", wait_x1o)
        out1[...] = buf["x1o"][...].reshape(out1.shape)
        arrived("x2o", wait_x2o)
        out2[...] = buf["x2o"][...].reshape(out2.shape)

    rows_sum("g3", mm("p3", jnp.concatenate(parts, axis=0), False), outputs)
    x3p, x3l = buf["x3p"], buf["x3l"]
    x3p[...] = mm("i3", rows_value("f3") - rows_value("g3"), False).reshape(x3p.shape)
    some = leaf_exchange("x3l", 2, lambda to: x3p.at[to], x3l, x3p[pos[2]])
    arrived("x3l", some)
    leaf_gather("x3o", 16, total(x3l, 2), buf["x3o"])
    out3[...] = buf["x3o"][...].reshape(out3.shape)

    for phase, whole in pending:
        remote(whole, whole, phase, {"rows": lax.rem(row + 1, NR)}).wait_send()


def store(*refs):
    copies = [pltpu.make_async_copy(refs[j], refs[4 + j], refs[8].at[j]) for j in range(4)]
    for copy in copies:
        copy.start()
    for copy in copies:
        copy.wait()


def body(*args):
    vmem = pl.BlockSpec(memory_space=pltpu.VMEM)
    smem = pl.BlockSpec(memory_space=pltpu.SMEM)
    outs = tuple(jax.ShapeDtypeStruct(item.shape, F32) for item in args[:4])
    solved = tuple(
        pl.pallas_call(
            kernel,
            out_shape=outs,
            in_specs=[pl.BlockSpec(memory_space=pltpu.MemorySpace.HBM)] * 11 + [smem] * 3,
            out_specs=[vmem] * 4,
            scratch_shapes=[pltpu.VMEM(BUFS[name], F32) for name in BUF_NAMES]
            + [pltpu.VMEM(shape, BF16) for _, shape in WEIGHTS] * 2
            + [pltpu.VMEM(shape, F32) for _, shape in WEIGHTS]
            + [pltpu.VMEM(shape, F32) for shape in RIGHT]
            + [pltpu.VMEM((2, 128, 128), BF16)] * 2
            + [pltpu.VMEM((NR, 8, N), jnp.int32), pltpu.SMEM((NR, 8, N), jnp.int32)]
            + [pltpu.SemaphoreType.DMA((11,)), pltpu.SemaphoreType.DMA]
            + [pltpu.SemaphoreType.DMA((len(PHASES),)), pltpu.SemaphoreType.DMA((len(PHASES),))],
            compiler_params=pltpu.CompilerParams(
                collective_id=0, has_side_effects=True, vmem_limit_bytes=60 * 1024 * 1024
            ),
        )(*args[:11], *(item.T for item in args[11:]))
    )
    return tuple(
        pl.pallas_call(
            store,
            out_shape=outs,
            in_specs=[vmem] * 4,
            out_specs=[pl.BlockSpec(memory_space=pltpu.MemorySpace.HBM)] * 4,
            scratch_shapes=[pltpu.SemaphoreType.DMA((4,))],
        )(*solved)
    )


def solution(mesh):
    rhs = P(None, "rows", None)
    return jax.shard_map(
        body,
        mesh=mesh,
        in_specs=(rhs,) * 4
        + (P("rows", "leaf"),) * 4
        + (P("leaf", "rows"),) * 3
        + (P(None, "rows"),) * 3,
        out_specs=(rhs,) * 4,
        check_vma=False,
    )
```

```python
import jax
import jax.numpy as jnp
from jax import lax
from jax.experimental import pallas as pl
from jax.experimental.pallas import tpu as pltpu
from jax.sharding import PartitionSpec as P

F32 = jnp.float32
BF16 = jnp.bfloat16
NR = 16
NL = 16
N = 128
MESH = pl.DeviceIdType.MESH

BUFS = {}
PHASES = []


def _pair(name, m):
    BUFS["c_" + name] = (8, m, N)
    BUFS["d_" + name] = (8, m, N)
    PHASES.append(name + "_c")


def _rows_ar(name, m):
    if m == 32:
        BUFS["a_" + name] = (8, 2, m, N)
        BUFS["b_" + name] = (8, m, N)
        BUFS["y_" + name] = (8, 2, m, N)
        _pair(name + "_rs", m)
        PHASES.append(name + "_ag_c")
    else:
        BUFS["a_" + name] = (NR, m, N)
        BUFS["b_" + name] = (NR, m, N)
        BUFS["y_" + name] = (NR, m, N)
    PHASES.extend([name + "_rs", name + "_ag"])


for _name, _m in (("f3", 32), ("f2", 32), ("f1", 16), ("f0", 16), ("g3", 32)):
    _rows_ar(_name, _m)
for _name, _g, _h in (("two", 4, 32), ("one", 8, 16), ("top", 16, 16)):
    if _h == 32:
        _pair(_name + "_rs", _h)
    BUFS["n_" + _name] = (8, 2, _h, N) if _h == 32 else (NR, _h, N)
    BUFS["m_" + _name] = (8, _h, N) if _h == 32 else (NR, _h, N)
    BUFS["w_" + _name] = (16 if _g == 8 else _g, _h, N)
    PHASES.extend([_name + "_rs", _name + "_ag"])
BUFS.update(
    u3=(2, 8, 16, N),
    u2=(2, 8, 16, N),
    ru32=(4, 2, 2, 16, N),
    ru31=(8, 2, 16, N),
    ru21=(8, 2, 16, N),
    ru30=(16, 2, 16, N),
    ru20=(16, 2, 16, N),
    bins0=(NR, 16, N),
    bins1=(NR, 16, N),
    pg=(8, 256, N),
    ph=(8, 256, N),
    wp0=(8, 16, 8, N),
    wp1=(8, 16, 8, N),
    ws0=(16, 8, 8, N),
    ws1=(16, 8, 8, N),
    nt=(NR, 2, 8, N),
    mt=(NR, 2, 8, N),
    wt=(16, 2, 8, N),
    x0p=(2, 16, 8, N),
    x0l=(16, 2, 8, N),
    x0r=(NR, 2, 8, N),
    x0o=(16, 2, 8, N),
    qg=(8, N, 512),
    qh=(8, N, 512),
    vp0=(8, 2, 8, 16, N),
    vp1=(8, 2, 8, 16, N),
    vs0=(8, 4, 2, 16, N),
    vs1=(8, 4, 2, 16, N),
    vs2=(8, 4, 2, 16, N),
    vs3=(8, 4, 2, 16, N),
    vr=(NR, 2, 2, 16, N),
    vt=(NR, 2, 2, 16, N),
    x0e=(2, NR, 2, 8, N),
    ch2=(2, 32, 16, N),
    s30=(8, 2, 8, N),
    t30=(16, 2, 8, N),
    x1p=(2, 8, 16, N),
    x1l=(16, 16, N),
    x1r=(NR, 16, N),
    x1o=(16, 16, N),
    s31=(4, 2, 16, N),
    t31=(8, 2, 16, N),
    x2p=(2, 4, 32, N),
    x2l=(8, 32, N),
    x2r=(8, 2, 32, N),
    x2o=(16, 32, N),
    s32=(2, 2, 32, N),
    t32=(4, 2, 32, N),
    x3o=(16, 64, N),
)
PHASES.extend(("u32", "u31", "u21", "u30", "u20", "x0l", "x0r", "x0o", "t30", "tag", "nt", "wt", "x0e", "vt"))
PHASES.extend(("up1", "up2", "up3", "up4", "dn1", "dn2", "dn3", "pc", "ws0", "ws1"))
PHASES.extend("q%s%d%s" % (way, step, half) for way in ("up", "dn") for step in range(1, 5) for half in "ab")
PHASES.extend(("qc", "vs0", "vs1", "vs2", "vs3"))
PHASES.extend(("x1l", "x1r", "x1o", "t31", "x2l", "x2r", "x2o", "t32", "x3o", "x2r_c"))
BUF_NAMES = list(BUFS)
PHASE_ID = {name: at for at, name in enumerate(PHASES)}
WEIGHTS = (
    ("i0", (256, 256)),
    ("i1", (128, 256)),
    ("i2", (128, 512)),
    ("i3", (64, 512)),
    ("p1", (256, 128)),
    ("p2", (512, 256)),
    ("p3", (512, 256)),
)
RIGHT = ((256, N), (2, 128, N), (128, N), (64, N))


def split(value):
    high = value.astype(BF16)
    return high, (value - high.astype(F32)).astype(BF16)


def kernel(*refs):
    rhs_in = refs[:4]
    weight_in = dict(zip([name for name, _ in WEIGHTS], refs[4:11]))
    r1, r2, r3 = refs[11:14]
    out0, out1, out2, out3 = refs[14:18]
    buf = dict(zip(BUF_NAMES, refs[18 : 18 + len(BUF_NAMES)]))
    at = 18 + len(BUF_NAMES)
    whi = dict(zip([name for name, _ in WEIGHTS], refs[at : at + 7]))
    wlo = dict(zip([name for name, _ in WEIGHTS], refs[at + 7 : at + 14]))
    w32 = dict(zip([name for name, _ in WEIGHTS], refs[at + 14 : at + 21]))
    rhs = refs[at + 21 : at + 25]
    w1hi, w1lo, w2hi, w2lo, p2hi, p2lo, tag, tag_s, load_sem, tag_sem, send_sem, recv_sem = refs[at + 25 :]

    leaf = lax.axis_index("leaf")
    row = lax.axis_index("rows")
    q1, q2, q3 = lax.div(leaf, 8), lax.div(leaf, 4), lax.div(leaf, 2)
    def eighth(at):
        return 2 * lax.rem(at, 8) + lax.div(at, 8)

    mine8 = eighth(leaf)
    pos = {16: leaf, 8: lax.rem(leaf, 8), 4: lax.rem(leaf, 4), 2: lax.rem(leaf, 2)}

    loads = {}

    def load(name, src, dst):
        loads[name] = pltpu.make_async_copy(src, dst, load_sem.at[len(loads)])
        loads[name].start()

    load("i3", weight_in["i3"], w32["i3"])
    for at, sep in ((3, q3), (2, q2), (0, 0)):
        load(at, rhs_in[at].at[sep], rhs[at])
    load(1, rhs_in[1], rhs[1])
    for name in ("p1", "p3", "i2", "p2", "i1", "i0"):
        load(name, weight_in[name], w32[name])

    def ready(*names):
        for name in names:
            loads[name].wait()
            whi[name][...], wlo[name][...] = split(w32[name][...])

    z, core = lax.div(row, 2), lax.rem(row, 2)
    partner = {"rows": row + 1 - 2 * core}

    def z_peer(step):
        half = lax.div(step + 1, 2)
        sign = 1 - 2 * lax.rem(step, 2)
        return lax.rem(z + 4 + half * sign, 8)

    def row_peer(step):
        half = lax.div(step + 1, 2)
        sign = 1 - 2 * lax.rem(step, 2)
        return lax.rem(row + 8 + half * sign, NR)

    barrier = pltpu.get_barrier_semaphore()

    def hello(step, carry):
        pl.semaphore_signal(barrier, inc=1, device_id={"rows": lax.rem(row + 1 + step, NR)}, device_id_type=MESH)
        pl.semaphore_signal(barrier, inc=1, device_id={"leaf": lax.rem(leaf + 1 + step, NL)}, device_id_type=MESH)
        return carry

    lax.fori_loop(0, 15, hello, 0)

    pending = []

    def remote(src, dst, phase, device):
        return pltpu.make_async_remote_copy(
            src_ref=src,
            dst_ref=dst,
            send_sem=send_sem.at[PHASE_ID[phase]],
            recv_sem=recv_sem.at[PHASE_ID[phase]],
            device_id=device,
            device_id_type=MESH,
        )

    def rows_send(phase, src, dst, whole):
        def go(step, carry):
            peer = row_peer(step)
            remote(src(peer), dst, phase, {"rows": peer}).start()
            return carry

        lax.fori_loop(0, NR - 1, go, 0)
        pending.append((phase, whole))

    def leaf_send(phase, group, src, dst, whole):
        base = leaf - pos[group]

        def go(step, carry):
            to = lax.rem(pos[group] + 1 + step, group)
            remote(src(to), dst, phase, {"leaf": base + to}).start()
            return carry

        lax.fori_loop(0, group - 1, go, 0)
        pending.append((phase, whole))

    def arrived(phase, whole):
        remote(whole, whole, phase, {"rows": lax.rem(row + 1, NR)}).wait_recv()

    def product(high, low, x, transposed):
        xh, xl = split(x)
        both = jnp.concatenate([xh, xl], axis=1)
        dims = (((0,), (0,)), ((), ())) if transposed else (((1,), (0,)), ((), ()))
        first = lax.dot_general(high, both, dims, preferred_element_type=F32)
        second = lax.dot_general(low, xh, dims, preferred_element_type=F32)
        return first[:, :N] + first[:, N:] + second

    def mm(name, x, transposed):
        return product(whi[name][...], wlo[name][...], x, transposed)

    pg, ph = buf["pg"], buf["ph"]
    z_up, z_down = lax.rem(z + 1, 8), lax.rem(z + 7, 8)

    def ring(step, own, land, mark):
        up, down = mark + "up%d", mark + "dn%d"
        if step > 1:
            arrived(up % (step - 1), land.at[0])
            arrived(down % (step - 1), land.at[0])
        at = lax.rem(z + 9 - step, 8)
        src = own if step == 1 else land.at[at]
        remote(src, land.at[at], up % step, {"rows": 2 * z_up + core}).start()
        pending.append((up % step, land.at[0]))
        if step < 4:
            at = lax.rem(z + step - 1, 8)
            src = own if step == 1 else land.at[at]
            remote(src, land.at[at], down % step, {"rows": 2 * z_down + core}).start()
            pending.append((down % step, land.at[0]))

    def ring_end(own, land, other, mark):
        arrived(mark + "up4", land.at[0])
        land[z] = own[...]
        remote(land, other, mark + "c" if mark else "pc", partner).start()
        pending.append((mark + "c" if mark else "pc", land))

    def relay(step):
        ring(step, w32["p1"], pg, "")

    qg, qh = buf["qg"], buf["qh"]

    def relay_two(step, half):
        some, name = pl.ds(64 * half, 64), "ab"[half]
        if step > 1:
            arrived("qup%d%s" % (step - 1, name), qg.at[0, some])
            arrived("qdn%d%s" % (step - 1, name), qg.at[0, some])
        for way, at, to in (("up", z + 9 - step, z_up), ("dn", z + step - 1, z_down)):
            if step == 4 and (way == "up") != (half == 0):
                continue
            mark = "q%s%d%s" % (way, step, name)
            land = qg.at[lax.rem(at, 8), some]
            src = w32["i2"].at[some] if step == 1 else land
            remote(src, land, mark, {"rows": 2 * to + core}).start()
            pending.append((mark, qg.at[0, some]))

    def relay_two_end():
        arrived("qup4a", qg.at[0, pl.ds(0, 64)])
        arrived("qdn4b", qg.at[0, pl.ds(64, 64)])
        qg[z] = w32["i2"][...]
        remote(qg, qh, "qc", partner).start()
        pending.append(("qc", qg))

    def chip_at(step):
        half = lax.div(step + 1, 2)
        sign = 2 * lax.rem(step, 2) - 1
        return lax.rem(z + 8 + half * sign, 8)

    def composite_two(source, out):
        dims = (((1,), (1,)), ((), ()))

        def one(at, carry):
            ih, il = split(source[chip_at(at)])
            first = lax.dot_general(
                p2hi[...], jnp.concatenate([ih, il], axis=0), dims, preferred_element_type=F32
            )
            second = lax.dot_general(p2lo[...], ih, dims, preferred_element_type=F32)
            out[at] = (first[:, :N] + first[:, N:] + second).reshape(2, 8, 16, N)
            return carry

        lax.fori_loop(0, 8, one, 0)

    parts_two = []

    def exchange_two(out, half):
        phase = "vs%d" % len(parts_two)
        some = pl.ds(4 * half, 4)
        parts_two.append(
            leaf_exchange(
                phase, 8, lambda to: out.at[some, :, to], buf[phase], out[some, :, pos[8]]
            )
        )

    vp0, vp1 = buf["vp0"], buf["vp1"]

    vr, vt = buf["vr"], buf["vt"]
    vt_all = vt.at[pl.ds(0, NR - 1)]
    pending.append(("vt", vt_all))

    def sum_two(j):
        arrived("vs%d" % j, parts_two[j])
        vs = buf["vs%d" % j]
        side = core if j < 2 else 1 - core
        for i in range(4):
            to = 2 * chip_at(jnp.int32(4 * (j % 2) + i)) + side
            for p in range(2):
                terms = [vs[4 * p + leaf_at, i] for leaf_at in range(4)]
                vr[to, p] = (terms[0] + terms[1]) + (terms[2] + terms[3])
            if j > 0 or i > 0:
                remote(vr.at[to], vt.at[row], "vt", {"rows": to}).start()

    def composite(source, out, phase):
        def one(at, carry):
            part = product(whi["i1"][...], wlo["i1"][...], source[at], False)
            out[at] = part.T.reshape(16, 8, N)
            return carry

        lax.fori_loop(0, 8, one, 0)
        return leaf_exchange(phase, 16, lambda to: out.at[:, eighth(to)], buf[phase], out[:, mine8])

    def total(ref, count):
        terms = [ref[j] for j in range(count)]
        while len(terms) > 1:
            terms = [a + b for a, b in zip(terms[::2], terms[1::2])]
        return terms[0]

    def z_send(phase, src, dst, whole):
        def go(step, carry):
            peer = z_peer(step)
            remote(src(peer), dst, phase, {"rows": 2 * peer + core}).start()
            return carry

        lax.fori_loop(0, 7, go, 0)
        pending.append((phase, whole))

    def pair_reduce(phase, out, land, fill=None):
        other, both = buf["c_" + phase], buf["d_" + phase]
        remote(out.at[:, 1 - core], other, phase + "_c", partner).start()
        pending.append((phase + "_c", other))
        arrived(phase + "_c", other)
        both[...] = out[:, core] + other[...]
        some = land.at[pl.ds(0, 7)]
        z_send(phase, lambda peer: both.at[peer], land.at[z], some)
        land[z] = both[z]
        if fill is not None:
            fill()
        arrived(phase, some)
        return total(land, 8)

    def pair_gather(phase, piece, full, fill=None):
        full[z, core] = piece
        some = full.at[pl.ds(0, 7), 0]
        z_send(phase, lambda peer: full.at[z, core], full.at[z, core], some)
        if fill is not None:
            fill()
        arrived(phase, some)
        mine = full.at[:, core]
        remote(mine, mine, phase + "_c", partner).start()
        pending.append((phase + "_c", mine))
        arrived(phase + "_c", mine)

    def rows_reduce(phase, out, land, fill=None):
        some = land.at[pl.ds(0, NR - 1)]
        rows_send(phase, lambda peer: out.at[peer], land.at[row], some)
        land[row] = out[row]
        if fill is not None:
            fill()
        arrived(phase, some)
        return total(land, NR)

    def rows_gather(phase, piece, full, fill=None):
        full[row] = piece
        some = full.at[pl.ds(0, NR - 1)]
        rows_send(phase, lambda peer: full.at[row], full.at[row], some)
        if fill is not None:
            fill()
        arrived(phase, some)

    def leaf_gather_start(phase, group, piece, full, slot=None):
        slot = pos[group] if slot is None else slot
        full[slot] = piece
        some = full.at[pl.ds(0, group - 1)]
        leaf_send(phase, group, lambda to: full.at[slot], full.at[slot], some)
        return some

    def leaf_gather(phase, group, piece, full):
        arrived(phase, leaf_gather_start(phase, group, piece, full))

    def leaf_exchange(phase, group, src, land, own, slot=None):
        slot = pos[group] if slot is None else slot
        some = land.at[pl.ds(0, group - 1)]
        leaf_send(phase, group, src, land.at[slot], some)
        land[slot] = own
        return some

    def rows_sum(name, value, fill=None, fill2=None):
        out, land, full = buf["a_" + name], buf["b_" + name], buf["y_" + name]
        out[...] = value.reshape(out.shape)
        paired = len(out.shape) == 4
        piece = (pair_reduce if paired else rows_reduce)(name + "_rs", out, land, fill)
        (pair_gather if paired else rows_gather)(name + "_ag", piece, full, fill2)

    def rows_value(name):
        full = buf["y_" + name]
        return full[...].reshape(-1, N)

    ready("i3")
    loads[3].wait()
    first = mm("i3", rhs[3][...], True)
    pl.semaphore_wait(barrier, 30)

    def ready_two():
        ready("i2", "p2")
        loads[2].wait()
        loads[1].wait()
        loads[0].wait()

    def send_tags():
        here = lax.broadcasted_iota(jnp.int32, (8, N), 1)
        value = jnp.where(here == 0, r1[0, 0], r1[0, 1])
        for p in range(4):
            for k in range(2):
                value = jnp.where(here == 2 + 2 * p + k, r2[k, p], value)
        tag[row] = value
        send_tags.some = tag.at[pl.ds(0, NR - 1)]
        rows_send("tag", lambda peer: tag.at[row], tag.at[row], send_tags.some)

    def slot_one():
        loads["p1"].wait()
        relay(1)
        send_tags()
        ready("p3")

    def slot_two():
        relay(2)
        ready_two()

    rows_sum("f3", first, slot_one, slot_two)
    u3 = buf["u3"]
    u3[...] = mm("p3", rows_value("f3"), True).reshape(u3.shape)
    ru32 = buf["ru32"]
    some = leaf_exchange(
        "u32", 4, lambda to: u3.at[:, pl.ds(2 * to, 2)], ru32, u3[:, pl.ds(2 * pos[4], 2)]
    )
    relay(3)
    arrived("u32", some)

    def bins(dst, terms, base, shape, add=None):
        for s in range(NR):
            value = None if add is None else add[s]
            for index, piece in terms:
                one = jnp.where(index == base(s), piece, jnp.zeros(shape, F32))
                value = one if value is None else value + one
            if len(dst.shape) == 4:
                dst[s // 2, s % 2] = value
            else:
                dst[s] = value

    terms = []
    for p in range(2):
        for k in range(2):
            piece = (ru32[2 * p, k] + ru32[2 * p + 1, k]).reshape(32, N)
            terms.append((r3[k, 2 * q2 + p], piece))
    bins(buf["n_two"], terms, lambda s: 48 + s, (32, N))

    ru31, ru30 = buf["ru31"], buf["ru30"]

    def start_u3_upper():
        start_u3_upper.one = leaf_exchange("u31", 8, lambda to: u3.at[:, to], ru31, u3[:, pos[8]])
        start_u3_upper.top = leaf_exchange(
            "u30", 16, lambda to: u3.at[:, lax.rem(to, 8)], ru30, u3[:, pos[8]]
        )
        relay(4)
        ready("i1", "i0")

    piece = pair_reduce("two_rs", buf["n_two"], buf["m_two"], start_u3_upper)
    some = leaf_gather_start("two_ag", 4, piece, buf["w_two"])
    ring_end(w32["p1"], pg, ph, "")
    relay_two(1, 0)
    relay_two(1, 1)
    arrived("two_ag", some)
    source = rhs[2][...] - buf["w_two"][...].reshape(128, N)

    def fill_one():
        arrived("u31", start_u3_upper.one)
        terms = []
        for p in range(4):
            for k in range(2):
                terms.append((r3[k, 4 * q1 + p], ru31[2 * p, k] + ru31[2 * p + 1, k]))
        bins(buf["bins1"], terms, lambda s: 32 + s, (16, N))

    def fill_top():
        arrived("u30", start_u3_upper.top)
        terms = []
        for p in range(8):
            for k in range(2):
                terms.append((r3[k, p], ru30[2 * p, k] + ru30[2 * p + 1, k]))
        bins(buf["bins0"], terms, lambda s: 2 * s + q1, (16, N))

    def slot_three():
        relay_two(2, 0)
        slot_three.some = composite(pg, buf["wp0"], "ws0")

    def slot_four():
        relay_two(2, 1)
        arrived("pc", ph)
        slot_four.some = composite(ph, buf["wp1"], "ws1")
        fill_top()

    rows_sum("f2", mm("i2", source, True), slot_three, slot_four)
    u2 = buf["u2"]
    u2[...] = mm("p2", rows_value("f2"), True).reshape(u2.shape)
    ru21, ru20 = buf["ru21"], buf["ru20"]
    some = leaf_exchange("u21", 8, lambda to: u2.at[:, to], ru21, u2[:, pos[8]])
    some_top = leaf_exchange("u20", 16, lambda to: u2.at[:, lax.rem(to, 8)], ru20, u2[:, pos[8]])
    relay_two(3, 0)
    relay_two(3, 1)
    p2hi[...], p2lo[...] = split(w32["p2"][...].T)
    fill_one()
    arrived("u21", some)
    terms = []
    for p in range(2):
        for k in range(2):
            piece = (ru21[4 * p, k] + ru21[4 * p + 1, k]) + (ru21[4 * p + 2, k] + ru21[4 * p + 3, k])
            terms.append((r2[k, 2 * q1 + p], piece))
    bins(buf["n_one"], terms, lambda s: 32 + s, (16, N), buf["bins1"])

    def fill_top_two():
        relay_two(4, 0)
        relay_two(4, 1)
        arrived("u20", some_top)
        terms = []
        for p in range(4):
            for k in range(2):
                piece = (ru20[4 * p, k] + ru20[4 * p + 1, k]) + (ru20[4 * p + 2, k] + ru20[4 * p + 3, k])
                terms.append((r2[k, p], piece))
        bins(buf["n_top"], terms, lambda s: 2 * s + q1, (16, N), buf["bins0"])
        ws0, ws1 = buf["ws0"], buf["ws1"]
        arrived("ws0", slot_three.some)
        arrived("ws1", slot_four.some)
        for p in range(2):
            halves = []
            for ws in (ws0, ws1):
                half = ws[8 * p]
                for j in range(1, 8):
                    half = half + ws[8 * p + j]
                halves.append(half.reshape(64, N))
            high, low = split(jnp.concatenate(halves, axis=0))
            w1hi[p] = high
            w1lo[p] = low
        arrived("tag", send_tags.some)
        copy = pltpu.make_async_copy(tag, tag_s, tag_sem)
        copy.start()
        copy.wait()

    piece = rows_reduce("one_rs", buf["n_one"], buf["m_one"], fill_top_two)
    n_top, m_top = buf["n_top"], buf["m_top"]
    some_one = leaf_gather_start("one_ag", 16, piece, buf["w_one"])
    some_top = m_top.at[pl.ds(0, NR - 1)]
    rows_send("top_rs", lambda peer: n_top.at[peer], m_top.at[row], some_top)
    m_top[row] = n_top[row]
    relay_two_end()
    composite_two(qg, vp0)
    arrived("one_ag", some_one)
    source = [rhs[1][p] - buf["w_one"][pl.ds(8 * p, 8)].reshape(128, N) for p in range(2)]

    def listed(p, k):
        return tag_s[k, 0, p]

    def block_at(j):
        return 2 * lax.rem(jnp.int32(j), 8) + (core if j < 8 else 1 - core)

    indices = [[listed(p, block_at(j)) for j in range(16)] for p in range(2)]
    terms = []
    for p in range(2):
        update = product(w1hi[p], w1lo[p], source[p], False)
        terms.extend((indices[p][j], update[8 * j : 8 * j + 8]) for j in range(16))
    nt = buf["nt"]
    for s in range(NR):
        for half in range(2):
            value = None
            for index, piece in terms:
                one = jnp.where(index == 2 * s + half, piece, jnp.zeros((8, N), F32))
                value = one if value is None else value + one
            nt[s, half] = value

    f1a, f1b = buf["a_f1"], buf["b_f1"]
    some_f1 = f1b.at[pl.ds(0, NR - 1)]

    def start_y1():
        exchange_two(vp0, 0)
        arrived("top_rs", some_top)
        start_y1.top = leaf_gather_start("top_ag", 16, total(m_top, NR), buf["w_top"])
        mine = jnp.where(q1 == 0, source[0], source[1])
        f1a[...] = mm("i1", mine, True).reshape(f1a.shape)
        rows_send("f1_rs", lambda peer: f1a.at[peer], f1b.at[row], some_f1)
        f1b[row] = f1a[row]
        arrived("qc", qh)
        composite_two(qh, vp1)

    piece = rows_reduce("nt", nt, buf["mt"], start_y1)
    wt = buf["wt"]
    some = leaf_gather_start("wt", 16, piece, wt, mine8)
    sum_two(0)
    arrived("top_ag", start_y1.top)
    arrived("wt", some)
    owed = jnp.concatenate([wt[:, 0].reshape(128, N), wt[:, 1].reshape(128, N)], axis=0)
    source = rhs[0][...] - (buf["w_top"][...].reshape(256, N) + owed)

    f1y = buf["y_f1"]

    def gather_y1():
        exchange_two(vp0, 1)
        arrived("f1_rs", some_f1)
        f1y[row] = total(f1b, NR)
        gather_y1.some = f1y.at[pl.ds(0, NR - 1)]
        rows_send("f1_ag", lambda peer: f1y.at[row], f1y.at[row], gather_y1.some)

    def solve_y1():
        exchange_two(vp1, 0)
        arrived("f1_ag", gather_y1.some)
        solve_y1.value = mm("i1", rows_value("f1"), False)

    rows_sum("f0", mm("i0", source, True), gather_y1, solve_y1)
    x0p, x0l, x0r = buf["x0p"], buf["x0l"], buf["x0r"]
    x0p[...] = mm("i0", rows_value("f0"), False).reshape(x0p.shape)
    some = leaf_exchange("x0l", 16, lambda to: x0p.at[:, eighth(to)], x0l, x0p[:, mine8])
    sum_two(1)
    sum_two(2)
    arrived("x0l", some)
    piece = total(x0l, 16)
    rows_gather("x0r", piece, x0r, lambda: exchange_two(vp1, 1))

    def pick_top(index):
        at = jnp.minimum(index, 31)
        held = x0r[lax.div(at, 2), lax.rem(at, 2)]
        return jnp.where(index < 32, held, jnp.zeros((8, N), F32))

    x1p = buf["x1p"]
    for p in range(2):
        chosen = jnp.concatenate([pick_top(indices[p][j]) for j in range(16)], axis=0)
        x1p[p] = -product(w1hi[p], w1lo[p], chosen, True).reshape(8, 16, N)
    x1p[q1] = x1p[q1] + solve_y1.value.reshape(8, 16, N)
    x1l, x1r = buf["x1l"], buf["x1r"]
    some = leaf_exchange("x1l", 16, lambda to: x1p.at[lax.div(to, 8), lax.rem(to, 8)], x1l, x1p[q1, pos[8]])
    wait_x0o = leaf_gather_start("x0o", 16, piece, buf["x0o"], mine8)
    x0e, ch2 = buf["x0e"], buf["ch2"]
    remote(x0r, x0e.at[q1], "x0e", {"leaf": lax.rem(leaf + 8, 16)}).start()
    pending.append(("x0e", x0e.at[0]))
    x0e[q1] = x0r[...]

    sum_two(3)
    s30, t30 = buf["s30"], buf["t30"]
    for p in range(8):
        for k in range(2):
            s30[p, k] = pick_top(r3[k, p])
    arrived("x1l", some)
    piece = total(x1l, 16)

    indices_two = [
        [tag_s[k // 2, 0, 2 + 2 * (2 * q1 + p) + k % 2] for k in range(32)] for p in range(2)
    ]

    def fill_t():
        fill_t.three = leaf_exchange("t30", 16, lambda to: s30.at[lax.div(to, 2)], t30, s30[q3], mine8)
        fill_t.own = mm("i2", rows_value("f2"), False)
        arrived("x0e", x0e.at[0])
        for p in range(2):
            for k in range(32):
                at = jnp.minimum(indices_two[p][k], 31)
                for half in range(2):
                    ch2[p, k, pl.ds(8 * half, 8)] = x0e[half, lax.div(at, 2), lax.rem(at, 2)]
        vt[row] = vr[row]
        arrived("vt", vt_all)
        for p in range(2):
            w2hi[p], w2lo[p] = split(vt[:, p].reshape(512, N))

    rows_gather("x1r", piece, x1r, fill_t)

    def pick_one(index):
        held = x1r[jnp.clip(index - 32, 0, 15)]
        mine = jnp.logical_and(index >= 32, index < 48)
        return jnp.where(mine, held, jnp.zeros((16, N), F32))

    x2p, x2l, x2r = buf["x2p"], buf["x2l"], buf["x2r"]
    for p in range(2):
        for k in range(32):
            index = indices_two[p][k]
            ch2[p, k] = jnp.where(index < 32, ch2[p, k], x1r[jnp.clip(index - 32, 0, 15)])
        x2p[p] = -product(w2hi[p], w2lo[p], ch2[p].reshape(512, N), True).reshape(4, 32, N)
    x2p[q2 - 2 * q1] = x2p[q2 - 2 * q1] + fill_t.own.reshape(4, 32, N)
    some = leaf_exchange(
        "x2l", 8, lambda to: x2p.at[lax.div(to, 4), lax.rem(to, 4)], x2l, x2p[q2 - 2 * q1, pos[4]]
    )
    wait_x1o = leaf_gather_start("x1o", 16, piece, buf["x1o"])
    s31, t31 = buf["s31"], buf["t31"]
    for p in range(4):
        for k in range(2):
            s31[p, k] = pick_one(r3[k, 4 * q1 + p])
    wait_t31 = leaf_exchange("t31", 8, lambda to: s31.at[lax.div(to, 2)], t31, s31[q3 - 4 * q1])
    arrived("x2l", some)
    piece = total(x2l, 8)
    pair_gather("x2r", piece, x2r)

    def pick_two(index):
        at = jnp.clip(index - 48, 0, 15)
        held = x2r[lax.div(at, 2), lax.rem(at, 2)]
        return jnp.where(index >= 48, held, jnp.zeros((32, N), F32))

    s32, t32 = buf["s32"], buf["t32"]
    for p in range(2):
        for k in range(2):
            s32[p, k] = pick_two(r3[k, 2 * q2 + p])
    some = leaf_exchange("t32", 4, lambda to: s32.at[lax.div(to, 2)], t32, s32[q3 - 2 * q2])
    wait_x2o = leaf_gather_start("x2o", 16, piece, buf["x2o"])
    arrived("t30", fill_t.three)
    arrived("t31", wait_t31)
    arrived("t32", some)
    parts = []
    for k in range(2):
        upper = t30[:, k].reshape(128, N) + t31[:, k].reshape(128, N)
        parts.append(upper + t32[:, k].reshape(128, N))

    def outputs():
        arrived("x0o", wait_x0o)
        for half in range(2):
            out0[0, pl.ds(128 * half, 128)] = buf["x0o"][:, half].reshape(128, N)
        arrived("x1o", wait_x1o)
        out1[...] = buf["x1o"][...].reshape(out1.shape)
        arrived("x2o", wait_x2o)
        out2[...] = buf["x2o"][...].reshape(out2.shape)

    rows_sum("g3", mm("p3", jnp.concatenate(parts, axis=0), False), outputs)
    x3o = buf["x3o"]
    part = mm("i3", rows_value("f3") - rows_value("g3"), False)
    arrived("x3o", leaf_gather_start("x3o", 16, part, x3o))
    for p in range(8):
        out3[p] = x3o[2 * p] + x3o[2 * p + 1]

    for phase, whole in pending:
        remote(whole, whole, phase, {"rows": lax.rem(row + 1, NR)}).wait_send()


def store(*refs):
    copies = [pltpu.make_async_copy(refs[j], refs[4 + j], refs[8].at[j]) for j in range(4)]
    for copy in copies:
        copy.start()
    for copy in copies:
        copy.wait()


def body(*args):
    vmem = pl.BlockSpec(memory_space=pltpu.VMEM)
    smem = pl.BlockSpec(memory_space=pltpu.SMEM)
    outs = tuple(jax.ShapeDtypeStruct(item.shape, F32) for item in args[:4])
    solved = tuple(
        pl.pallas_call(
            kernel,
            out_shape=outs,
            in_specs=[pl.BlockSpec(memory_space=pltpu.MemorySpace.HBM)] * 11 + [smem] * 3,
            out_specs=[vmem] * 4,
            scratch_shapes=[pltpu.VMEM(BUFS[name], F32) for name in BUF_NAMES]
            + [pltpu.VMEM(shape, BF16) for _, shape in WEIGHTS] * 2
            + [pltpu.VMEM(shape, F32) for _, shape in WEIGHTS]
            + [pltpu.VMEM(shape, F32) for shape in RIGHT]
            + [pltpu.VMEM((2, 128, 128), BF16)] * 2
            + [pltpu.VMEM((2, 512, 128), BF16)] * 2
            + [pltpu.VMEM((256, 512), BF16)] * 2
            + [pltpu.VMEM((NR, 8, N), jnp.int32), pltpu.SMEM((NR, 8, N), jnp.int32)]
            + [pltpu.SemaphoreType.DMA((11,)), pltpu.SemaphoreType.DMA]
            + [pltpu.SemaphoreType.DMA((len(PHASES),)), pltpu.SemaphoreType.DMA((len(PHASES),))],
            compiler_params=pltpu.CompilerParams(
                collective_id=0, has_side_effects=True, vmem_limit_bytes=60 * 1024 * 1024
            ),
        )(*args[:11], *(item.T for item in args[11:]))
    )
    return tuple(
        pl.pallas_call(
            store,
            out_shape=outs,
            in_specs=[vmem] * 4,
            out_specs=[pl.BlockSpec(memory_space=pltpu.MemorySpace.HBM)] * 4,
            scratch_shapes=[pltpu.SemaphoreType.DMA((4,))],
        )(*solved)
    )


def solution(mesh):
    rhs = P(None, "rows", None)
    return jax.shard_map(
        body,
        mesh=mesh,
        in_specs=(rhs,) * 4
        + (P("rows", "leaf"),) * 4
        + (P("leaf", "rows"),) * 3
        + (P(None, "rows"),) * 3,
        out_specs=(rhs,) * 4,
        check_vma=False,
    )
```

```python
import jax
import jax.numpy as jnp
from jax import lax
from jax.experimental import pallas as pl
from jax.experimental.pallas import tpu as pltpu
from jax.sharding import PartitionSpec as P

F32 = jnp.float32
BF16 = jnp.bfloat16
NR = 16
NL = 16
N = 128
MESH = pl.DeviceIdType.MESH

BUFS = {}
PHASES = []


def _pair(name, m):
    BUFS["c_" + name] = (8, m, N)
    BUFS["d_" + name] = (8, m, N)
    PHASES.append(name + "_c")


def _rows_ar(name, m):
    if m == 32:
        BUFS["a_" + name] = (8, 2, m, N)
        BUFS["b_" + name] = (8, m, N)
        BUFS["y_" + name] = (8, 2, m, N)
        _pair(name + "_rs", m)
        PHASES.append(name + "_ag_c")
    else:
        BUFS["a_" + name] = (NR, m, N)
        BUFS["b_" + name] = (NR, m, N)
        BUFS["y_" + name] = (NR, m, N)
    PHASES.extend([name + "_rs", name + "_ag"])


for _name, _m in (("f3", 32), ("f2", 32), ("f1", 16), ("f0", 16), ("g3", 32)):
    _rows_ar(_name, _m)
for _name, _g, _h in (("two", 4, 32), ("one", 8, 16), ("top", 16, 16)):
    if _h == 32:
        _pair(_name + "_rs", _h)
    BUFS["n_" + _name] = (8, 2, _h, N) if _h == 32 else (NR, _h, N)
    BUFS["m_" + _name] = (8, _h, N) if _h == 32 else (NR, _h, N)
    BUFS["w_" + _name] = (16 if _g == 8 else _g, _h, N)
    PHASES.extend([_name + "_rs", _name + "_ag"])
BUFS.update(
    u3=(2, 8, 16, N),
    u2=(2, 8, 16, N),
    ru32=(4, 2, 2, 16, N),
    ru31=(8, 2, 16, N),
    ru21=(8, 2, 16, N),
    ru30=(16, 2, 16, N),
    ru20=(16, 2, 16, N),
    bins0=(NR, 16, N),
    bins1=(NR, 16, N),
    pg=(8, 256, N),
    ph=(8, 256, N),
    wp0=(8, 16, 8, N),
    wp1=(8, 16, 8, N),
    ws0=(16, 8, 8, N),
    ws1=(16, 8, 8, N),
    nt=(NR, 2, 8, N),
    mt=(NR, 2, 8, N),
    wt=(16, 2, 8, N),
    x0p=(2, 16, 8, N),
    x0l=(16, 2, 8, N),
    x0r=(NR, 2, 8, N),
    x0o=(16, 2, 8, N),
    qg=(8, N, 512),
    qh=(8, N, 512),
    vp0=(8, 2, 8, 16, N),
    vp1=(8, 2, 8, 16, N),
    vs0=(8, 4, 2, 16, N),
    vs1=(8, 4, 2, 16, N),
    vs2=(8, 4, 2, 16, N),
    vs3=(8, 4, 2, 16, N),
    vr=(NR, 2, 2, 16, N),
    vt=(NR, 2, 2, 16, N),
    x0e=(2, NR, 2, 8, N),
    ch2=(2, 32, 16, N),
    s30=(8, 2, 8, N),
    t30=(16, 2, 8, N),
    x1p=(2, 8, 16, N),
    x1l=(16, 16, N),
    x1r=(NR, 16, N),
    x1o=(16, 16, N),
    s31=(4, 2, 16, N),
    t31=(8, 2, 16, N),
    x2p=(2, 4, 32, N),
    x2l=(8, 32, N),
    x2r=(8, 2, 32, N),
    x2o=(16, 32, N),
    s32=(2, 2, 32, N),
    t32=(4, 2, 32, N),
    x3o=(16, 64, N),
)
PHASES.extend(("u32", "u31", "u21", "u30", "u20", "x0l", "x0r", "x0o", "t30", "tag", "nt", "wt", "x0e", "vt"))
PHASES.extend(("up1", "up2", "up3", "up4", "dn1", "dn2", "dn3", "pc", "ws0", "ws1"))
PHASES.extend("q%s%d%s" % (way, step, half) for way in ("up", "dn") for step in range(1, 5) for half in "ab")
PHASES.extend(("qc", "vs0", "vs1", "vs2", "vs3"))
PHASES.extend(("x1l", "x1r", "x1o", "t31", "x2l", "x2r", "x2o", "t32", "x3o", "x2r_c"))
BUF_NAMES = list(BUFS)
PHASE_ID = {name: at for at, name in enumerate(PHASES)}
WEIGHTS = (
    ("i0", (256, 256)),
    ("i1", (128, 256)),
    ("i2", (128, 512)),
    ("i3", (64, 512)),
    ("p1", (256, 128)),
    ("p2", (512, 256)),
    ("p3", (512, 256)),
)
RIGHT = ((256, N), (2, 128, N), (128, N), (64, N))


def split(value):
    high = value.astype(BF16)
    return high, (value - high.astype(F32)).astype(BF16)


def kernel(*refs):
    rhs_in = refs[:4]
    weight_in = dict(zip([name for name, _ in WEIGHTS], refs[4:11]))
    r1, r2, r3 = refs[11:14]
    out0, out1, out2, out3 = refs[14:18]
    buf = dict(zip(BUF_NAMES, refs[18 : 18 + len(BUF_NAMES)]))
    at = 18 + len(BUF_NAMES)
    whi = dict(zip([name for name, _ in WEIGHTS], refs[at : at + 7]))
    wlo = dict(zip([name for name, _ in WEIGHTS], refs[at + 7 : at + 14]))
    w32 = dict(zip([name for name, _ in WEIGHTS], refs[at + 14 : at + 21]))
    rhs = refs[at + 21 : at + 25]
    w1hi, w1lo, w2hi, w2lo, p2hi, p2lo, p3hi, p3lo, i2hi, i2lo, i0hi, i0lo, tag, tag_s, load_sem, tag_sem, send_sem, recv_sem = refs[at + 25 :]

    leaf = lax.axis_index("leaf")
    row = lax.axis_index("rows")
    q1, q2, q3 = lax.div(leaf, 8), lax.div(leaf, 4), lax.div(leaf, 2)
    def eighth(at):
        return 2 * lax.rem(at, 8) + lax.div(at, 8)

    mine8 = eighth(leaf)
    pos = {16: leaf, 8: lax.rem(leaf, 8), 4: lax.rem(leaf, 4), 2: lax.rem(leaf, 2)}

    loads = {}

    def load(name, src, dst):
        loads[name] = pltpu.make_async_copy(src, dst, load_sem.at[len(loads)])
        loads[name].start()

    load("i3", weight_in["i3"], w32["i3"])
    for at, sep in ((3, q3), (2, q2), (0, 0)):
        load(at, rhs_in[at].at[sep], rhs[at])
    load(1, rhs_in[1], rhs[1])
    for name in ("p1", "p3", "i2", "p2", "i1", "i0"):
        load(name, weight_in[name], w32[name])

    def ready(*names):
        for name in names:
            loads[name].wait()
            whi[name][...], wlo[name][...] = split(w32[name][...])

    z, core = lax.div(row, 2), lax.rem(row, 2)
    partner = {"rows": row + 1 - 2 * core}

    def z_peer(step):
        half = lax.div(step + 1, 2)
        sign = 1 - 2 * lax.rem(step, 2)
        return lax.rem(z + 4 + half * sign, 8)

    def row_peer(step):
        half = lax.div(step + 1, 2)
        sign = 1 - 2 * lax.rem(step, 2)
        return lax.rem(row + 8 + half * sign, NR)

    barrier = pltpu.get_barrier_semaphore()

    def hello(step, carry):
        pl.semaphore_signal(barrier, inc=1, device_id={"rows": lax.rem(row + 1 + step, NR)}, device_id_type=MESH)
        pl.semaphore_signal(barrier, inc=1, device_id={"leaf": lax.rem(leaf + 1 + step, NL)}, device_id_type=MESH)
        return carry

    lax.fori_loop(0, 15, hello, 0)

    pending = []

    def remote(src, dst, phase, device):
        return pltpu.make_async_remote_copy(
            src_ref=src,
            dst_ref=dst,
            send_sem=send_sem.at[PHASE_ID[phase]],
            recv_sem=recv_sem.at[PHASE_ID[phase]],
            device_id=device,
            device_id_type=MESH,
        )

    def rows_send(phase, src, dst, whole):
        def go(step, carry):
            peer = row_peer(step)
            remote(src(peer), dst, phase, {"rows": peer}).start()
            return carry

        lax.fori_loop(0, NR - 1, go, 0)
        pending.append((phase, whole))

    def leaf_send(phase, group, src, dst, whole):
        base = leaf - pos[group]

        def go(step, carry):
            to = lax.rem(pos[group] + 1 + step, group)
            remote(src(to), dst, phase, {"leaf": base + to}).start()
            return carry

        lax.fori_loop(0, group - 1, go, 0)
        pending.append((phase, whole))

    def arrived(phase, whole):
        remote(whole, whole, phase, {"rows": lax.rem(row + 1, NR)}).wait_recv()

    def product(high, low, x, transposed):
        xh, xl = split(x)
        both = jnp.concatenate([xh, xl], axis=1)
        dims = (((0,), (0,)), ((), ())) if transposed else (((1,), (0,)), ((), ()))
        first = lax.dot_general(high, both, dims, preferred_element_type=F32)
        second = lax.dot_general(low, xh, dims, preferred_element_type=F32)
        return first[:, :N] + first[:, N:] + second

    def mm(name, x, transposed):
        return product(whi[name][...], wlo[name][...], x, transposed)

    pg, ph = buf["pg"], buf["ph"]
    z_up, z_down = lax.rem(z + 1, 8), lax.rem(z + 7, 8)

    def ring(step, own, land, mark):
        up, down = mark + "up%d", mark + "dn%d"
        if step > 1:
            arrived(up % (step - 1), land.at[0])
            arrived(down % (step - 1), land.at[0])
        at = lax.rem(z + 9 - step, 8)
        src = own if step == 1 else land.at[at]
        remote(src, land.at[at], up % step, {"rows": 2 * z_up + core}).start()
        pending.append((up % step, land.at[0]))
        if step < 4:
            at = lax.rem(z + step - 1, 8)
            src = own if step == 1 else land.at[at]
            remote(src, land.at[at], down % step, {"rows": 2 * z_down + core}).start()
            pending.append((down % step, land.at[0]))

    def ring_end(own, land, other, mark):
        arrived(mark + "up4", land.at[0])
        land[z] = own[...]
        remote(land, other, mark + "c" if mark else "pc", partner).start()
        pending.append((mark + "c" if mark else "pc", land))

    def relay(step):
        ring(step, w32["p1"], pg, "")

    qg, qh = buf["qg"], buf["qh"]

    def relay_two(step, half):
        some, name = pl.ds(64 * half, 64), "ab"[half]
        if step > 1:
            arrived("qup%d%s" % (step - 1, name), qg.at[0, some])
            arrived("qdn%d%s" % (step - 1, name), qg.at[0, some])
        for way, at, to in (("up", z + 9 - step, z_up), ("dn", z + step - 1, z_down)):
            if step == 4 and (way == "up") != (half == 0):
                continue
            mark = "q%s%d%s" % (way, step, name)
            land = qg.at[lax.rem(at, 8), some]
            src = w32["i2"].at[some] if step == 1 else land
            remote(src, land, mark, {"rows": 2 * to + core}).start()
            pending.append((mark, qg.at[0, some]))

    def relay_two_end():
        arrived("qup4a", qg.at[0, pl.ds(0, 64)])
        arrived("qdn4b", qg.at[0, pl.ds(64, 64)])
        qg[z] = w32["i2"][...]
        remote(qg, qh, "qc", partner).start()
        pending.append(("qc", qg))

    def chip_at(step):
        half = lax.div(step + 1, 2)
        sign = 2 * lax.rem(step, 2) - 1
        return lax.rem(z + 8 + half * sign, 8)

    def composite_two(source, out):
        dims = (((1,), (1,)), ((), ()))

        def one(at, carry):
            ih, il = split(source[chip_at(at)])
            first = lax.dot_general(
                p2hi[...], jnp.concatenate([ih, il], axis=0), dims, preferred_element_type=F32
            )
            second = lax.dot_general(p2lo[...], ih, dims, preferred_element_type=F32)
            out[at] = (first[:, :N] + first[:, N:] + second).reshape(2, 8, 16, N)
            return carry

        lax.fori_loop(0, 8, one, 0)

    parts_two = []

    def exchange_two(out, half):
        phase = "vs%d" % len(parts_two)
        some = pl.ds(4 * half, 4)
        parts_two.append(
            leaf_exchange(
                phase, 8, lambda to: out.at[some, :, to], buf[phase], out[some, :, pos[8]]
            )
        )

    vp0, vp1 = buf["vp0"], buf["vp1"]

    vr, vt = buf["vr"], buf["vt"]
    vt_all = vt.at[pl.ds(0, NR - 1)]
    pending.append(("vt", vt_all))

    def sum_two(j):
        arrived("vs%d" % j, parts_two[j])
        vs = buf["vs%d" % j]
        side = core if j < 2 else 1 - core
        for i in range(4):
            to = 2 * chip_at(jnp.int32(4 * (j % 2) + i)) + side
            for p in range(2):
                terms = [vs[4 * p + leaf_at, i] for leaf_at in range(4)]
                vr[to, p] = (terms[0] + terms[1]) + (terms[2] + terms[3])
            if j > 0 or i > 0:
                remote(vr.at[to], vt.at[row], "vt", {"rows": to}).start()

    def composite(source, out, phase):
        def one(at, carry):
            part = product(whi["i1"][...], wlo["i1"][...], source[at], False)
            out[at] = part.T.reshape(16, 8, N)
            return carry

        lax.fori_loop(0, 8, one, 0)
        return leaf_exchange(phase, 16, lambda to: out.at[:, eighth(to)], buf[phase], out[:, mine8])

    def total(ref, count):
        terms = [ref[j] for j in range(count)]
        while len(terms) > 1:
            terms = [a + b for a, b in zip(terms[::2], terms[1::2])]
        return terms[0]

    def z_send(phase, src, dst, whole):
        def go(step, carry):
            peer = z_peer(step)
            remote(src(peer), dst, phase, {"rows": 2 * peer + core}).start()
            return carry

        lax.fori_loop(0, 7, go, 0)
        pending.append((phase, whole))

    def pair_reduce(phase, out, land, fill=None):
        other, both = buf["c_" + phase], buf["d_" + phase]
        remote(out.at[:, 1 - core], other, phase + "_c", partner).start()
        pending.append((phase + "_c", other))
        arrived(phase + "_c", other)
        both[...] = out[:, core] + other[...]
        some = land.at[pl.ds(0, 7)]
        z_send(phase, lambda peer: both.at[peer], land.at[z], some)
        land[z] = both[z]
        if fill is not None:
            fill()
        arrived(phase, some)
        return total(land, 8)

    def pair_gather(phase, piece, full, fill=None):
        full[z, core] = piece
        some = full.at[pl.ds(0, 7), 0]
        z_send(phase, lambda peer: full.at[z, core], full.at[z, core], some)
        if fill is not None:
            fill()
        arrived(phase, some)
        mine = full.at[:, core]
        remote(mine, mine, phase + "_c", partner).start()
        pending.append((phase + "_c", mine))
        arrived(phase + "_c", mine)

    def rows_reduce(phase, out, land, fill=None):
        some = land.at[pl.ds(0, NR - 1)]
        rows_send(phase, lambda peer: out.at[peer], land.at[row], some)
        land[row] = out[row]
        if fill is not None:
            fill()
        arrived(phase, some)
        return total(land, NR)

    def rows_gather(phase, piece, full, fill=None):
        full[row] = piece
        some = full.at[pl.ds(0, NR - 1)]
        rows_send(phase, lambda peer: full.at[row], full.at[row], some)
        if fill is not None:
            fill()
        arrived(phase, some)

    def leaf_gather_start(phase, group, piece, full, slot=None):
        slot = pos[group] if slot is None else slot
        full[slot] = piece
        some = full.at[pl.ds(0, group - 1)]
        leaf_send(phase, group, lambda to: full.at[slot], full.at[slot], some)
        return some

    def leaf_gather(phase, group, piece, full):
        arrived(phase, leaf_gather_start(phase, group, piece, full))

    def leaf_exchange(phase, group, src, land, own, slot=None):
        slot = pos[group] if slot is None else slot
        some = land.at[pl.ds(0, group - 1)]
        leaf_send(phase, group, src, land.at[slot], some)
        land[slot] = own
        return some

    def rows_sum(name, value, fill=None, fill2=None):
        out, land, full = buf["a_" + name], buf["b_" + name], buf["y_" + name]
        out[...] = value.reshape(out.shape)
        paired = len(out.shape) == 4
        piece = (pair_reduce if paired else rows_reduce)(name + "_rs", out, land, fill)
        (pair_gather if paired else rows_gather)(name + "_ag", piece, full, fill2)

    def rows_value(name):
        full = buf["y_" + name]
        return full[...].reshape(-1, N)

    ready("i3")
    loads[3].wait()
    first = mm("i3", rhs[3][...], True)
    pl.semaphore_wait(barrier, 30)

    def ready_two():
        loads["i2"].wait()
        i2hi[...], i2lo[...] = split(w32["i2"][...].T)
        loads[2].wait()
        loads[1].wait()
        loads[0].wait()

    def send_tags():
        here = lax.broadcasted_iota(jnp.int32, (8, N), 1)
        value = jnp.where(here == 0, r1[0, 0], r1[0, 1])
        for p in range(4):
            for k in range(2):
                value = jnp.where(here == 2 + 2 * p + k, r2[k, p], value)
        tag[row] = value
        send_tags.some = tag.at[pl.ds(0, NR - 1)]
        rows_send("tag", lambda peer: tag.at[row], tag.at[row], send_tags.some)

    def slot_one():
        loads["p1"].wait()
        relay(1)
        send_tags()
        loads["p3"].wait()
        p3hi[...], p3lo[...] = split(w32["p3"][...].T)

    def slot_two():
        relay(2)
        ready_two()

    rows_sum("f3", first, slot_one, slot_two)
    u3 = buf["u3"]
    u3[...] = product(p3hi[...], p3lo[...], rows_value("f3"), False).reshape(u3.shape)
    ru32 = buf["ru32"]
    some = leaf_exchange(
        "u32", 4, lambda to: u3.at[:, pl.ds(2 * to, 2)], ru32, u3[:, pl.ds(2 * pos[4], 2)]
    )
    relay(3)
    arrived("u32", some)

    def bins(dst, terms, base, shape, add=None):
        for s in range(NR):
            value = None if add is None else add[s]
            for index, piece in terms:
                one = jnp.where(index == base(s), piece, jnp.zeros(shape, F32))
                value = one if value is None else value + one
            if len(dst.shape) == 4:
                dst[s // 2, s % 2] = value
            else:
                dst[s] = value

    terms = []
    for p in range(2):
        for k in range(2):
            piece = (ru32[2 * p, k] + ru32[2 * p + 1, k]).reshape(32, N)
            terms.append((r3[k, 2 * q2 + p], piece))
    bins(buf["n_two"], terms, lambda s: 48 + s, (32, N))

    ru31, ru30 = buf["ru31"], buf["ru30"]

    def start_u3_upper():
        start_u3_upper.one = leaf_exchange("u31", 8, lambda to: u3.at[:, to], ru31, u3[:, pos[8]])
        start_u3_upper.top = leaf_exchange(
            "u30", 16, lambda to: u3.at[:, lax.rem(to, 8)], ru30, u3[:, pos[8]]
        )
        relay(4)
        ready("i1")
        loads["p2"].wait()
        p2hi[...], p2lo[...] = split(w32["p2"][...].T)

    piece = pair_reduce("two_rs", buf["n_two"], buf["m_two"], start_u3_upper)
    some = leaf_gather_start("two_ag", 4, piece, buf["w_two"])
    ring_end(w32["p1"], pg, ph, "")
    relay_two(1, 0)
    relay_two(1, 1)
    arrived("two_ag", some)
    source = rhs[2][...] - buf["w_two"][...].reshape(128, N)

    def fill_one():
        arrived("u31", start_u3_upper.one)
        terms = []
        for p in range(4):
            for k in range(2):
                terms.append((r3[k, 4 * q1 + p], ru31[2 * p, k] + ru31[2 * p + 1, k]))
        bins(buf["bins1"], terms, lambda s: 32 + s, (16, N))

    def fill_top():
        arrived("u30", start_u3_upper.top)
        terms = []
        for p in range(8):
            for k in range(2):
                terms.append((r3[k, p], ru30[2 * p, k] + ru30[2 * p + 1, k]))
        bins(buf["bins0"], terms, lambda s: 2 * s + q1, (16, N))

    def slot_three():
        relay_two(2, 0)
        slot_three.some = composite(pg, buf["wp0"], "ws0")

    def slot_four():
        relay_two(2, 1)
        arrived("pc", ph)
        slot_four.some = composite(ph, buf["wp1"], "ws1")
        fill_top()

    rows_sum("f2", product(i2hi[...], i2lo[...], source, False), slot_three, slot_four)
    u2 = buf["u2"]
    u2[...] = product(p2hi[...], p2lo[...], rows_value("f2"), False).reshape(u2.shape)
    ru21, ru20 = buf["ru21"], buf["ru20"]
    some = leaf_exchange("u21", 8, lambda to: u2.at[:, to], ru21, u2[:, pos[8]])
    some_top = leaf_exchange("u20", 16, lambda to: u2.at[:, lax.rem(to, 8)], ru20, u2[:, pos[8]])
    relay_two(3, 0)
    relay_two(3, 1)
    ready("i0")
    i0hi[...], i0lo[...] = split(w32["i0"][...].T)
    fill_one()
    arrived("u21", some)
    terms = []
    for p in range(2):
        for k in range(2):
            piece = (ru21[4 * p, k] + ru21[4 * p + 1, k]) + (ru21[4 * p + 2, k] + ru21[4 * p + 3, k])
            terms.append((r2[k, 2 * q1 + p], piece))
    bins(buf["n_one"], terms, lambda s: 32 + s, (16, N), buf["bins1"])

    def fill_top_two():
        relay_two(4, 0)
        relay_two(4, 1)
        arrived("u20", some_top)
        terms = []
        for p in range(4):
            for k in range(2):
                piece = (ru20[4 * p, k] + ru20[4 * p + 1, k]) + (ru20[4 * p + 2, k] + ru20[4 * p + 3, k])
                terms.append((r2[k, p], piece))
        bins(buf["n_top"], terms, lambda s: 2 * s + q1, (16, N), buf["bins0"])
        ws0, ws1 = buf["ws0"], buf["ws1"]
        arrived("ws0", slot_three.some)
        arrived("ws1", slot_four.some)
        for p in range(2):
            halves = []
            for ws in (ws0, ws1):
                half = ws[8 * p]
                for j in range(1, 8):
                    half = half + ws[8 * p + j]
                halves.append(half.reshape(64, N))
            high, low = split(jnp.concatenate(halves, axis=0))
            w1hi[p] = high
            w1lo[p] = low
        arrived("tag", send_tags.some)
        copy = pltpu.make_async_copy(tag, tag_s, tag_sem)
        copy.start()
        copy.wait()

    piece = rows_reduce("one_rs", buf["n_one"], buf["m_one"], fill_top_two)
    n_top, m_top = buf["n_top"], buf["m_top"]
    some_one = leaf_gather_start("one_ag", 16, piece, buf["w_one"])
    some_top = m_top.at[pl.ds(0, NR - 1)]
    rows_send("top_rs", lambda peer: n_top.at[peer], m_top.at[row], some_top)
    m_top[row] = n_top[row]
    relay_two_end()
    composite_two(qg, vp0)
    arrived("one_ag", some_one)
    source = [rhs[1][p] - buf["w_one"][pl.ds(8 * p, 8)].reshape(128, N) for p in range(2)]

    def listed(p, k):
        return tag_s[k, 0, p]

    def block_at(j):
        return 2 * lax.rem(jnp.int32(j), 8) + (core if j < 8 else 1 - core)

    indices = [[listed(p, block_at(j)) for j in range(16)] for p in range(2)]
    terms = []
    for p in range(2):
        update = product(w1hi[p], w1lo[p], source[p], False)
        terms.extend((indices[p][j], update[8 * j : 8 * j + 8]) for j in range(16))
    nt = buf["nt"]
    for s in range(NR):
        for half in range(2):
            value = None
            for index, piece in terms:
                one = jnp.where(index == 2 * s + half, piece, jnp.zeros((8, N), F32))
                value = one if value is None else value + one
            nt[s, half] = value

    f1a, f1b = buf["a_f1"], buf["b_f1"]
    some_f1 = f1b.at[pl.ds(0, NR - 1)]

    def start_y1():
        exchange_two(vp0, 0)
        arrived("top_rs", some_top)
        start_y1.top = leaf_gather_start("top_ag", 16, total(m_top, NR), buf["w_top"])
        mine = jnp.where(q1 == 0, source[0], source[1])
        f1a[...] = mm("i1", mine, True).reshape(f1a.shape)
        rows_send("f1_rs", lambda peer: f1a.at[peer], f1b.at[row], some_f1)
        f1b[row] = f1a[row]
        arrived("qc", qh)
        composite_two(qh, vp1)

    piece = rows_reduce("nt", nt, buf["mt"], start_y1)
    wt = buf["wt"]
    some = leaf_gather_start("wt", 16, piece, wt, mine8)
    sum_two(0)
    arrived("top_ag", start_y1.top)
    arrived("wt", some)
    owed = jnp.concatenate([wt[:, 0].reshape(128, N), wt[:, 1].reshape(128, N)], axis=0)
    source = rhs[0][...] - (buf["w_top"][...].reshape(256, N) + owed)

    f1y = buf["y_f1"]

    def gather_y1():
        exchange_two(vp0, 1)
        arrived("f1_rs", some_f1)
        f1y[row] = total(f1b, NR)
        gather_y1.some = f1y.at[pl.ds(0, NR - 1)]
        rows_send("f1_ag", lambda peer: f1y.at[row], f1y.at[row], gather_y1.some)

    def solve_y1():
        exchange_two(vp1, 0)
        whi["i2"][...], wlo["i2"][...] = split(w32["i2"][...])
        whi["p3"][...], wlo["p3"][...] = split(w32["p3"][...])
        arrived("f1_ag", gather_y1.some)
        solve_y1.value = mm("i1", rows_value("f1"), False)

    rows_sum("f0", product(i0hi[...], i0lo[...], source, False), gather_y1, solve_y1)
    x0p, x0l, x0r = buf["x0p"], buf["x0l"], buf["x0r"]
    x0p[...] = mm("i0", rows_value("f0"), False).reshape(x0p.shape)
    some = leaf_exchange("x0l", 16, lambda to: x0p.at[:, eighth(to)], x0l, x0p[:, mine8])
    sum_two(1)
    sum_two(2)
    arrived("x0l", some)
    piece = total(x0l, 16)
    rows_gather("x0r", piece, x0r, lambda: exchange_two(vp1, 1))

    def pick_top(index):
        at = jnp.minimum(index, 31)
        held = x0r[lax.div(at, 2), lax.rem(at, 2)]
        return jnp.where(index < 32, held, jnp.zeros((8, N), F32))

    x1p = buf["x1p"]
    for p in range(2):
        chosen = jnp.concatenate([pick_top(indices[p][j]) for j in range(16)], axis=0)
        x1p[p] = -product(w1hi[p], w1lo[p], chosen, True).reshape(8, 16, N)
    x1p[q1] = x1p[q1] + solve_y1.value.reshape(8, 16, N)
    x1l, x1r = buf["x1l"], buf["x1r"]
    some = leaf_exchange("x1l", 16, lambda to: x1p.at[lax.div(to, 8), lax.rem(to, 8)], x1l, x1p[q1, pos[8]])
    piece_top = piece
    x0e, ch2 = buf["x0e"], buf["ch2"]
    remote(x0r, x0e.at[q1], "x0e", {"leaf": lax.rem(leaf + 8, 16)}).start()
    pending.append(("x0e", x0e.at[0]))
    x0e[q1] = x0r[...]

    sum_two(3)
    s30, t30 = buf["s30"], buf["t30"]
    for p in range(8):
        for k in range(2):
            s30[p, k] = pick_top(r3[k, p])
    arrived("x1l", some)
    piece = total(x1l, 16)

    indices_two = [
        [tag_s[k // 2, 0, 2 + 2 * (2 * q1 + p) + k % 2] for k in range(32)] for p in range(2)
    ]

    def fill_t():
        fill_t.out = leaf_gather_start("x0o", 16, piece_top, buf["x0o"], mine8)
        fill_t.three = leaf_exchange("t30", 16, lambda to: s30.at[lax.div(to, 2)], t30, s30[q3], mine8)
        fill_t.own = mm("i2", rows_value("f2"), False)
        arrived("x0e", x0e.at[0])
        for p in range(2):
            for k in range(32):
                at = jnp.minimum(indices_two[p][k], 31)
                for half in range(2):
                    ch2[p, k, pl.ds(8 * half, 8)] = x0e[half, lax.div(at, 2), lax.rem(at, 2)]
        vt[row] = vr[row]
        arrived("vt", vt_all)
        for p in range(2):
            w2hi[p], w2lo[p] = split(vt[:, p].reshape(512, N))

    rows_gather("x1r", piece, x1r, fill_t)

    def pick_one(index):
        held = x1r[jnp.clip(index - 32, 0, 15)]
        mine = jnp.logical_and(index >= 32, index < 48)
        return jnp.where(mine, held, jnp.zeros((16, N), F32))

    x2p, x2l, x2r = buf["x2p"], buf["x2l"], buf["x2r"]
    for p in range(2):
        for k in range(32):
            index = indices_two[p][k]
            ch2[p, k] = jnp.where(index < 32, ch2[p, k], x1r[jnp.clip(index - 32, 0, 15)])
        x2p[p] = -product(w2hi[p], w2lo[p], ch2[p].reshape(512, N), True).reshape(4, 32, N)
    x2p[q2 - 2 * q1] = x2p[q2 - 2 * q1] + fill_t.own.reshape(4, 32, N)
    some = leaf_exchange(
        "x2l", 8, lambda to: x2p.at[lax.div(to, 4), lax.rem(to, 4)], x2l, x2p[q2 - 2 * q1, pos[4]]
    )
    piece_one = piece
    s31, t31 = buf["s31"], buf["t31"]
    for p in range(4):
        for k in range(2):
            s31[p, k] = pick_one(r3[k, 4 * q1 + p])
    arrived("x2l", some)
    piece = total(x2l, 8)

    def fill_o():
        fill_o.three = leaf_exchange("t31", 8, lambda to: s31.at[lax.div(to, 2)], t31, s31[q3 - 4 * q1])
        fill_o.out = leaf_gather_start("x1o", 16, piece_one, buf["x1o"])

    pair_gather("x2r", piece, x2r, fill_o)

    def pick_two(index):
        at = jnp.clip(index - 48, 0, 15)
        held = x2r[lax.div(at, 2), lax.rem(at, 2)]
        return jnp.where(index >= 48, held, jnp.zeros((32, N), F32))

    s32, t32 = buf["s32"], buf["t32"]
    for p in range(2):
        for k in range(2):
            s32[p, k] = pick_two(r3[k, 2 * q2 + p])
    some = leaf_exchange("t32", 4, lambda to: s32.at[lax.div(to, 2)], t32, s32[q3 - 2 * q2])
    piece_two = piece
    arrived("t30", fill_t.three)
    arrived("t31", fill_o.three)
    arrived("t32", some)
    parts = []
    for k in range(2):
        upper = t30[:, k].reshape(128, N) + t31[:, k].reshape(128, N)
        parts.append(upper + t32[:, k].reshape(128, N))

    def last_out():
        last_out.some = leaf_gather_start("x2o", 16, piece_two, buf["x2o"])

    def outputs():
        arrived("x0o", fill_t.out)
        for half in range(2):
            out0[0, pl.ds(128 * half, 128)] = buf["x0o"][:, half].reshape(128, N)
        arrived("x1o", fill_o.out)
        out1[...] = buf["x1o"][...].reshape(out1.shape)
        arrived("x2o", last_out.some)
        out2[...] = buf["x2o"][...].reshape(out2.shape)

    rows_sum("g3", mm("p3", jnp.concatenate(parts, axis=0), False), last_out, outputs)
    x3o = buf["x3o"]
    part = mm("i3", rows_value("f3") - rows_value("g3"), False)
    arrived("x3o", leaf_gather_start("x3o", 16, part, x3o))
    for p in range(8):
        out3[p] = x3o[2 * p] + x3o[2 * p + 1]

    for phase, whole in pending:
        remote(whole, whole, phase, {"rows": lax.rem(row + 1, NR)}).wait_send()


def store(*refs):
    copies = [pltpu.make_async_copy(refs[j], refs[4 + j], refs[8].at[j]) for j in range(4)]
    for copy in copies:
        copy.start()
    for copy in copies:
        copy.wait()


def body(*args):
    vmem = pl.BlockSpec(memory_space=pltpu.VMEM)
    smem = pl.BlockSpec(memory_space=pltpu.SMEM)
    outs = tuple(jax.ShapeDtypeStruct(item.shape, F32) for item in args[:4])
    solved = tuple(
        pl.pallas_call(
            kernel,
            out_shape=outs,
            in_specs=[pl.BlockSpec(memory_space=pltpu.MemorySpace.HBM)] * 11 + [smem] * 3,
            out_specs=[vmem] * 4,
            scratch_shapes=[pltpu.VMEM(BUFS[name], F32) for name in BUF_NAMES]
            + [pltpu.VMEM(shape, BF16) for _, shape in WEIGHTS] * 2
            + [pltpu.VMEM(shape, F32) for _, shape in WEIGHTS]
            + [pltpu.VMEM(shape, F32) for shape in RIGHT]
            + [pltpu.VMEM((2, 128, 128), BF16)] * 2
            + [pltpu.VMEM((2, 512, 128), BF16)] * 2
            + [pltpu.VMEM((256, 512), BF16)] * 4
            + [pltpu.VMEM((512, 128), BF16)] * 2
            + [pltpu.VMEM((256, 256), BF16)] * 2
            + [pltpu.VMEM((NR, 8, N), jnp.int32), pltpu.SMEM((NR, 8, N), jnp.int32)]
            + [pltpu.SemaphoreType.DMA((11,)), pltpu.SemaphoreType.DMA]
            + [pltpu.SemaphoreType.DMA((len(PHASES),)), pltpu.SemaphoreType.DMA((len(PHASES),))],
            compiler_params=pltpu.CompilerParams(
                collective_id=0, has_side_effects=True, vmem_limit_bytes=60 * 1024 * 1024
            ),
        )(*args[:11], *(item.T for item in args[11:]))
    )
    return tuple(
        pl.pallas_call(
            store,
            out_shape=outs,
            in_specs=[vmem] * 4,
            out_specs=[pl.BlockSpec(memory_space=pltpu.MemorySpace.HBM)] * 4,
            scratch_shapes=[pltpu.SemaphoreType.DMA((4,))],
        )(*solved)
    )


def solution(mesh):
    rhs = P(None, "rows", None)
    return jax.shard_map(
        body,
        mesh=mesh,
        in_specs=(rhs,) * 4
        + (P("rows", "leaf"),) * 4
        + (P("leaf", "rows"),) * 3
        + (P(None, "rows"),) * 3,
        out_specs=(rhs,) * 4,
        check_vma=False,
    )
```

```python
import jax
import jax.numpy as jnp
from jax import lax
from jax.experimental import pallas as pl
from jax.experimental.pallas import tpu as pltpu
from jax.sharding import PartitionSpec as P

F32 = jnp.float32
BF16 = jnp.bfloat16
NR = 16
NL = 16
N = 128
MESH = pl.DeviceIdType.MESH

BUFS = {}
PHASES = []


def _pair(name, m):
    BUFS["c_" + name] = (8, m, N)
    BUFS["d_" + name] = (8, m, N)
    PHASES.append(name + "_c")


def _rows_ar(name, m):
    if m == 32:
        BUFS["a_" + name] = (8, 2, m, N)
        BUFS["b_" + name] = (8, m, N)
        BUFS["y_" + name] = (8, 2, m, N)
        _pair(name + "_rs", m)
        PHASES.append(name + "_ag_c")
    else:
        BUFS["a_" + name] = (NR, m, N)
        BUFS["b_" + name] = (NR, m, N)
        BUFS["y_" + name] = (NR, m, N)
    PHASES.extend([name + "_rs", name + "_ag"])


for _name, _m in (("f3", 32), ("f2", 32), ("f1", 16), ("f0", 16), ("g3", 32)):
    _rows_ar(_name, _m)
for _name, _g, _h in (("two", 4, 32), ("one", 8, 16), ("top", 16, 16)):
    if _h == 32:
        _pair(_name + "_rs", _h)
    BUFS["n_" + _name] = (8, 2, _h, N) if _h == 32 else (NR, _h, N)
    BUFS["m_" + _name] = (8, _h, N) if _h == 32 else (NR, _h, N)
    BUFS["w_" + _name] = (16 if _g == 8 else _g, _h, N)
    PHASES.extend([_name + "_rs", _name + "_ag"])
BUFS.update(
    u3=(2, 8, 16, N),
    u2=(2, 8, 16, N),
    ru32=(4, 2, 2, 16, N),
    ru31=(8, 2, 16, N),
    ru21=(8, 2, 16, N),
    ru30=(16, 2, 16, N),
    ru20=(16, 2, 16, N),
    bins0=(NR, 16, N),
    bins1=(NR, 16, N),
    pg=(8, 256, N),
    ph=(8, 256, N),
    wp0=(8, 16, 8, N),
    wp1=(8, 16, 8, N),
    ws0=(16, 8, 8, N),
    ws1=(16, 8, 8, N),
    nt=(NR, 2, 8, N),
    mt=(NR, 2, 8, N),
    wt=(16, 2, 8, N),
    x0p=(2, 16, 8, N),
    x0l=(16, 2, 8, N),
    x0r=(NR, 2, 8, N),
    x0o=(16, 2, 8, N),
    qg=(8, N, 512),
    qh=(8, N, 512),
    vp0=(8, 2, 8, 16, N),
    vp1=(8, 2, 8, 16, N),
    vs0=(8, 4, 2, 16, N),
    vs1=(8, 4, 2, 16, N),
    vs2=(8, 4, 2, 16, N),
    vs3=(8, 4, 2, 16, N),
    vr=(NR, 2, 2, 16, N),
    vt=(NR, 2, 2, 16, N),
    x0e=(2, NR, 2, 8, N),
    ch2=(2, 32, 16, N),
    s30=(8, 2, 8, N),
    t30=(16, 2, 8, N),
    x1p=(2, 8, 16, N),
    x1l=(16, 16, N),
    x1r=(NR, 16, N),
    x1o=(16, 16, N),
    s31=(4, 2, 16, N),
    t31=(8, 2, 16, N),
    x2p=(2, 4, 32, N),
    x2l=(8, 32, N),
    x2r=(8, 2, 32, N),
    x2o=(16, 32, N),
    s32=(2, 2, 32, N),
    t32=(4, 2, 32, N),
    x3o=(16, 64, N),
)
PHASES.extend(("u32", "u31", "u21", "u30", "u20", "x0l", "x0r", "x0o", "t30", "tag", "nt", "wt", "x0e", "vt"))
PHASES.extend(("up1", "up2", "up3", "up4", "dn1", "dn2", "dn3", "pc", "ws0", "ws1"))
PHASES.extend("q%s%d%s" % (way, step, half) for way in ("up", "dn") for step in range(1, 5) for half in "ab")
PHASES.extend(("qc", "vs0", "vs1", "vs2", "vs3"))
PHASES.extend(("x1l", "x1r", "x1o", "t31", "x2l", "x2r", "x2o", "t32", "x3o", "x2r_c"))
BUF_NAMES = list(BUFS)
PHASE_ID = {name: at for at, name in enumerate(PHASES)}
WEIGHTS = (
    ("i0", (256, 256)),
    ("i1", (128, 256)),
    ("i2", (128, 512)),
    ("i3", (64, 512)),
    ("p1", (256, 128)),
    ("p2", (512, 256)),
    ("p3", (512, 256)),
)
RIGHT = ((256, N), (2, 128, N), (128, N), (64, N))


def split(value):
    high = value.astype(BF16)
    return high, (value - high.astype(F32)).astype(BF16)


def kernel(*refs):
    rhs_in = refs[:4]
    weight_in = dict(zip([name for name, _ in WEIGHTS], refs[4:11]))
    r1, r2, r3 = refs[11:14]
    out0, out1, out2, out3 = refs[14:18]
    buf = dict(zip(BUF_NAMES, refs[18 : 18 + len(BUF_NAMES)]))
    at = 18 + len(BUF_NAMES)
    whi = dict(zip([name for name, _ in WEIGHTS], refs[at : at + 7]))
    wlo = dict(zip([name for name, _ in WEIGHTS], refs[at + 7 : at + 14]))
    w32 = dict(zip([name for name, _ in WEIGHTS], refs[at + 14 : at + 21]))
    rhs = refs[at + 21 : at + 25]
    w1hi, w1lo, w2hi, w2lo, p2hi, p2lo, p3hi, p3lo, i2hi, i2lo, i0hi, i0lo, tag, tag_s, load_sem, tag_sem, send_sem, recv_sem = refs[at + 25 :]

    leaf = lax.axis_index("leaf")
    row = lax.axis_index("rows")
    q1, q2, q3 = lax.div(leaf, 8), lax.div(leaf, 4), lax.div(leaf, 2)
    def eighth(at):
        return 2 * lax.rem(at, 8) + lax.div(at, 8)

    mine8 = eighth(leaf)
    pos = {16: leaf, 8: lax.rem(leaf, 8), 4: lax.rem(leaf, 4), 2: lax.rem(leaf, 2)}

    loads = {}

    def load(name, src, dst):
        loads[name] = pltpu.make_async_copy(src, dst, load_sem.at[len(loads)])
        loads[name].start()

    load("i3", weight_in["i3"], w32["i3"])
    for at, sep in ((3, q3), (2, q2), (0, 0)):
        load(at, rhs_in[at].at[sep], rhs[at])
    load(1, rhs_in[1], rhs[1])
    for name in ("p1", "p3", "i2", "p2", "i1", "i0"):
        load(name, weight_in[name], w32[name])

    def ready(*names):
        for name in names:
            loads[name].wait()
            whi[name][...], wlo[name][...] = split(w32[name][...])

    z, core = lax.div(row, 2), lax.rem(row, 2)
    partner = {"rows": row + 1 - 2 * core}

    def z_peer(step):
        half = lax.div(step + 1, 2)
        sign = 1 - 2 * lax.rem(step, 2)
        return lax.rem(z + 4 + half * sign, 8)

    def row_peer(step):
        half = lax.div(step + 1, 2)
        sign = 1 - 2 * lax.rem(step, 2)
        return lax.rem(row + 8 + half * sign, NR)

    barrier = pltpu.get_barrier_semaphore()

    def hello(step, carry):
        pl.semaphore_signal(barrier, inc=1, device_id={"rows": lax.rem(row + 1 + step, NR)}, device_id_type=MESH)
        pl.semaphore_signal(barrier, inc=1, device_id={"leaf": lax.rem(leaf + 1 + step, NL)}, device_id_type=MESH)
        return carry

    lax.fori_loop(0, 15, hello, 0)

    pending = []

    def remote(src, dst, phase, device):
        return pltpu.make_async_remote_copy(
            src_ref=src,
            dst_ref=dst,
            send_sem=send_sem.at[PHASE_ID[phase]],
            recv_sem=recv_sem.at[PHASE_ID[phase]],
            device_id=device,
            device_id_type=MESH,
        )

    def rows_send(phase, src, dst, whole):
        def go(step, carry):
            peer = row_peer(step)
            remote(src(peer), dst, phase, {"rows": peer}).start()
            return carry

        lax.fori_loop(0, NR - 1, go, 0, unroll=True)
        pending.append((phase, whole))

    def leaf_send(phase, group, src, dst, whole):
        base = leaf - pos[group]

        def go(step, carry):
            to = lax.rem(pos[group] + 1 + step, group)
            remote(src(to), dst, phase, {"leaf": base + to}).start()
            return carry

        lax.fori_loop(0, group - 1, go, 0, unroll=True)
        pending.append((phase, whole))

    def arrived(phase, whole):
        remote(whole, whole, phase, {"rows": lax.rem(row + 1, NR)}).wait_recv()

    def product(high, low, x, transposed):
        xh, xl = split(x)
        both = jnp.concatenate([xh, xl], axis=1)
        dims = (((0,), (0,)), ((), ())) if transposed else (((1,), (0,)), ((), ()))
        first = lax.dot_general(high, both, dims, preferred_element_type=F32)
        second = lax.dot_general(low, xh, dims, preferred_element_type=F32)
        return first[:, :N] + first[:, N:] + second

    def mm(name, x, transposed):
        return product(whi[name][...], wlo[name][...], x, transposed)

    pg, ph = buf["pg"], buf["ph"]
    z_up, z_down = lax.rem(z + 1, 8), lax.rem(z + 7, 8)

    def ring(step, own, land, mark):
        up, down = mark + "up%d", mark + "dn%d"
        if step > 1:
            arrived(up % (step - 1), land.at[0])
            arrived(down % (step - 1), land.at[0])
        at = lax.rem(z + 9 - step, 8)
        src = own if step == 1 else land.at[at]
        remote(src, land.at[at], up % step, {"rows": 2 * z_up + core}).start()
        pending.append((up % step, land.at[0]))
        if step < 4:
            at = lax.rem(z + step - 1, 8)
            src = own if step == 1 else land.at[at]
            remote(src, land.at[at], down % step, {"rows": 2 * z_down + core}).start()
            pending.append((down % step, land.at[0]))

    def ring_end(own, land, other, mark):
        arrived(mark + "up4", land.at[0])
        land[z] = own[...]
        remote(land, other, mark + "c" if mark else "pc", partner).start()
        pending.append((mark + "c" if mark else "pc", land))

    def relay(step):
        ring(step, w32["p1"], pg, "")

    qg, qh = buf["qg"], buf["qh"]

    def relay_two(step, half):
        some, name = pl.ds(64 * half, 64), "ab"[half]
        if step > 1:
            arrived("qup%d%s" % (step - 1, name), qg.at[0, some])
            arrived("qdn%d%s" % (step - 1, name), qg.at[0, some])
        for way, at, to in (("up", z + 9 - step, z_up), ("dn", z + step - 1, z_down)):
            if step == 4 and (way == "up") != (half == 0):
                continue
            mark = "q%s%d%s" % (way, step, name)
            land = qg.at[lax.rem(at, 8), some]
            src = w32["i2"].at[some] if step == 1 else land
            remote(src, land, mark, {"rows": 2 * to + core}).start()
            pending.append((mark, qg.at[0, some]))

    def relay_two_end():
        arrived("qup4a", qg.at[0, pl.ds(0, 64)])
        arrived("qdn4b", qg.at[0, pl.ds(64, 64)])
        qg[z] = w32["i2"][...]
        remote(qg, qh, "qc", partner).start()
        pending.append(("qc", qg))

    def chip_at(step):
        half = lax.div(step + 1, 2)
        sign = 2 * lax.rem(step, 2) - 1
        return lax.rem(z + 8 + half * sign, 8)

    def composite_two(source, out):
        dims = (((1,), (1,)), ((), ()))

        def one(at, carry):
            ih, il = split(source[chip_at(at)])
            first = lax.dot_general(
                p2hi[...], jnp.concatenate([ih, il], axis=0), dims, preferred_element_type=F32
            )
            second = lax.dot_general(p2lo[...], ih, dims, preferred_element_type=F32)
            out[at] = (first[:, :N] + first[:, N:] + second).reshape(2, 8, 16, N)
            return carry

        lax.fori_loop(0, 8, one, 0)

    parts_two = []

    def exchange_two(out, half):
        phase = "vs%d" % len(parts_two)
        some = pl.ds(4 * half, 4)
        parts_two.append(
            leaf_exchange(
                phase, 8, lambda to: out.at[some, :, to], buf[phase], out[some, :, pos[8]]
            )
        )

    vp0, vp1 = buf["vp0"], buf["vp1"]

    vr, vt = buf["vr"], buf["vt"]
    vt_all = vt.at[pl.ds(0, NR - 1)]
    pending.append(("vt", vt_all))

    def sum_two(j):
        arrived("vs%d" % j, parts_two[j])
        vs = buf["vs%d" % j]
        side = core if j < 2 else 1 - core
        for i in range(4):
            to = 2 * chip_at(jnp.int32(4 * (j % 2) + i)) + side
            for p in range(2):
                terms = [vs[4 * p + leaf_at, i] for leaf_at in range(4)]
                vr[to, p] = (terms[0] + terms[1]) + (terms[2] + terms[3])
            if j > 0 or i > 0:
                remote(vr.at[to], vt.at[row], "vt", {"rows": to}).start()

    def composite(source, out, phase):
        def one(at, carry):
            part = product(whi["i1"][...], wlo["i1"][...], source[at], False)
            out[at] = part.T.reshape(16, 8, N)
            return carry

        lax.fori_loop(0, 8, one, 0)
        return leaf_exchange(phase, 16, lambda to: out.at[:, eighth(to)], buf[phase], out[:, mine8])

    def total(ref, count):
        terms = [ref[j] for j in range(count)]
        while len(terms) > 1:
            terms = [a + b for a, b in zip(terms[::2], terms[1::2])]
        return terms[0]

    def z_send(phase, src, dst, whole):
        def go(step, carry):
            peer = z_peer(step)
            remote(src(peer), dst, phase, {"rows": 2 * peer + core}).start()
            return carry

        lax.fori_loop(0, 7, go, 0, unroll=True)
        pending.append((phase, whole))

    def pair_reduce(phase, out, land, fill=None):
        other, both = buf["c_" + phase], buf["d_" + phase]
        remote(out.at[:, 1 - core], other, phase + "_c", partner).start()
        pending.append((phase + "_c", other))
        arrived(phase + "_c", other)
        both[...] = out[:, core] + other[...]
        some = land.at[pl.ds(0, 7)]
        z_send(phase, lambda peer: both.at[peer], land.at[z], some)
        land[z] = both[z]
        if fill is not None:
            fill()
        arrived(phase, some)
        return total(land, 8)

    def pair_gather(phase, piece, full, fill=None):
        full[z, core] = piece
        some = full.at[pl.ds(0, 7), 0]
        z_send(phase, lambda peer: full.at[z, core], full.at[z, core], some)
        if fill is not None:
            fill()
        arrived(phase, some)
        mine = full.at[:, core]
        remote(mine, mine, phase + "_c", partner).start()
        pending.append((phase + "_c", mine))
        arrived(phase + "_c", mine)

    def rows_reduce(phase, out, land, fill=None):
        some = land.at[pl.ds(0, NR - 1)]
        rows_send(phase, lambda peer: out.at[peer], land.at[row], some)
        land[row] = out[row]
        if fill is not None:
            fill()
        arrived(phase, some)
        return total(land, NR)

    def rows_gather(phase, piece, full, fill=None):
        full[row] = piece
        some = full.at[pl.ds(0, NR - 1)]
        rows_send(phase, lambda peer: full.at[row], full.at[row], some)
        if fill is not None:
            fill()
        arrived(phase, some)

    def leaf_gather_start(phase, group, piece, full, slot=None):
        slot = pos[group] if slot is None else slot
        full[slot] = piece
        some = full.at[pl.ds(0, group - 1)]
        leaf_send(phase, group, lambda to: full.at[slot], full.at[slot], some)
        return some

    def leaf_gather(phase, group, piece, full):
        arrived(phase, leaf_gather_start(phase, group, piece, full))

    def leaf_exchange(phase, group, src, land, own, slot=None):
        slot = pos[group] if slot is None else slot
        some = land.at[pl.ds(0, group - 1)]
        leaf_send(phase, group, src, land.at[slot], some)
        land[slot] = own
        return some

    def rows_sum(name, value, fill=None, fill2=None):
        out, land, full = buf["a_" + name], buf["b_" + name], buf["y_" + name]
        out[...] = value.reshape(out.shape)
        paired = len(out.shape) == 4
        piece = (pair_reduce if paired else rows_reduce)(name + "_rs", out, land, fill)
        (pair_gather if paired else rows_gather)(name + "_ag", piece, full, fill2)

    def rows_value(name):
        full = buf["y_" + name]
        return full[...].reshape(-1, N)

    ready("i3")
    loads[3].wait()
    first = mm("i3", rhs[3][...], True)
    pl.semaphore_wait(barrier, 30)

    def ready_two():
        loads["i2"].wait()
        i2hi[...], i2lo[...] = split(w32["i2"][...].T)
        loads[2].wait()
        loads[1].wait()
        loads[0].wait()

    def send_tags():
        here = lax.broadcasted_iota(jnp.int32, (8, N), 1)
        value = jnp.where(here == 0, r1[0, 0], r1[0, 1])
        for p in range(4):
            for k in range(2):
                value = jnp.where(here == 2 + 2 * p + k, r2[k, p], value)
        tag[row] = value
        send_tags.some = tag.at[pl.ds(0, NR - 1)]
        rows_send("tag", lambda peer: tag.at[row], tag.at[row], send_tags.some)

    def slot_one():
        loads["p1"].wait()
        relay(1)
        send_tags()
        loads["p3"].wait()
        p3hi[...], p3lo[...] = split(w32["p3"][...].T)

    def slot_two():
        relay(2)
        ready_two()

    rows_sum("f3", first, slot_one, slot_two)
    u3 = buf["u3"]
    u3[...] = product(p3hi[...], p3lo[...], rows_value("f3"), False).reshape(u3.shape)
    ru32 = buf["ru32"]
    some = leaf_exchange(
        "u32", 4, lambda to: u3.at[:, pl.ds(2 * to, 2)], ru32, u3[:, pl.ds(2 * pos[4], 2)]
    )
    relay(3)
    arrived("u32", some)

    def bins(dst, terms, base, shape, add=None):
        for s in range(NR):
            value = None if add is None else add[s]
            for index, piece in terms:
                one = jnp.where(index == base(s), piece, jnp.zeros(shape, F32))
                value = one if value is None else value + one
            if len(dst.shape) == 4:
                dst[s // 2, s % 2] = value
            else:
                dst[s] = value

    terms = []
    for p in range(2):
        for k in range(2):
            piece = (ru32[2 * p, k] + ru32[2 * p + 1, k]).reshape(32, N)
            terms.append((r3[k, 2 * q2 + p], piece))
    bins(buf["n_two"], terms, lambda s: 48 + s, (32, N))

    ru31, ru30 = buf["ru31"], buf["ru30"]

    def start_u3_upper():
        start_u3_upper.one = leaf_exchange("u31", 8, lambda to: u3.at[:, to], ru31, u3[:, pos[8]])
        start_u3_upper.top = leaf_exchange(
            "u30", 16, lambda to: u3.at[:, lax.rem(to, 8)], ru30, u3[:, pos[8]]
        )
        relay(4)
        ready("i1")
        loads["p2"].wait()
        p2hi[...], p2lo[...] = split(w32["p2"][...].T)

    piece = pair_reduce("two_rs", buf["n_two"], buf["m_two"], start_u3_upper)
    some = leaf_gather_start("two_ag", 4, piece, buf["w_two"])
    ring_end(w32["p1"], pg, ph, "")
    relay_two(1, 0)
    relay_two(1, 1)
    arrived("two_ag", some)
    source = rhs[2][...] - buf["w_two"][...].reshape(128, N)

    def fill_one():
        arrived("u31", start_u3_upper.one)
        terms = []
        for p in range(4):
            for k in range(2):
                terms.append((r3[k, 4 * q1 + p], ru31[2 * p, k] + ru31[2 * p + 1, k]))
        bins(buf["bins1"], terms, lambda s: 32 + s, (16, N))

    def fill_top():
        arrived("u30", start_u3_upper.top)
        terms = []
        for p in range(8):
            for k in range(2):
                terms.append((r3[k, p], ru30[2 * p, k] + ru30[2 * p + 1, k]))
        bins(buf["bins0"], terms, lambda s: 2 * s + q1, (16, N))

    def slot_three():
        relay_two(2, 0)
        slot_three.some = composite(pg, buf["wp0"], "ws0")

    def slot_four():
        relay_two(2, 1)
        arrived("pc", ph)
        slot_four.some = composite(ph, buf["wp1"], "ws1")
        fill_top()

    rows_sum("f2", product(i2hi[...], i2lo[...], source, False), slot_three, slot_four)
    u2 = buf["u2"]
    u2[...] = product(p2hi[...], p2lo[...], rows_value("f2"), False).reshape(u2.shape)
    ru21, ru20 = buf["ru21"], buf["ru20"]
    some = leaf_exchange("u21", 8, lambda to: u2.at[:, to], ru21, u2[:, pos[8]])
    some_top = leaf_exchange("u20", 16, lambda to: u2.at[:, lax.rem(to, 8)], ru20, u2[:, pos[8]])
    relay_two(3, 0)
    relay_two(3, 1)
    ready("i0")
    i0hi[...], i0lo[...] = split(w32["i0"][...].T)
    fill_one()
    arrived("u21", some)
    terms = []
    for p in range(2):
        for k in range(2):
            piece = (ru21[4 * p, k] + ru21[4 * p + 1, k]) + (ru21[4 * p + 2, k] + ru21[4 * p + 3, k])
            terms.append((r2[k, 2 * q1 + p], piece))
    bins(buf["n_one"], terms, lambda s: 32 + s, (16, N), buf["bins1"])

    def fill_top_two():
        relay_two(4, 0)
        relay_two(4, 1)
        arrived("u20", some_top)
        terms = []
        for p in range(4):
            for k in range(2):
                piece = (ru20[4 * p, k] + ru20[4 * p + 1, k]) + (ru20[4 * p + 2, k] + ru20[4 * p + 3, k])
                terms.append((r2[k, p], piece))
        bins(buf["n_top"], terms, lambda s: 2 * s + q1, (16, N), buf["bins0"])
        ws0, ws1 = buf["ws0"], buf["ws1"]
        arrived("ws0", slot_three.some)
        arrived("ws1", slot_four.some)
        for p in range(2):
            halves = []
            for ws in (ws0, ws1):
                half = ws[8 * p]
                for j in range(1, 8):
                    half = half + ws[8 * p + j]
                halves.append(half.reshape(64, N))
            high, low = split(jnp.concatenate(halves, axis=0))
            w1hi[p] = high
            w1lo[p] = low
        arrived("tag", send_tags.some)
        copy = pltpu.make_async_copy(tag, tag_s, tag_sem)
        copy.start()
        copy.wait()

    piece = rows_reduce("one_rs", buf["n_one"], buf["m_one"], fill_top_two)
    n_top, m_top = buf["n_top"], buf["m_top"]
    some_one = leaf_gather_start("one_ag", 16, piece, buf["w_one"])
    some_top = m_top.at[pl.ds(0, NR - 1)]
    rows_send("top_rs", lambda peer: n_top.at[peer], m_top.at[row], some_top)
    m_top[row] = n_top[row]
    relay_two_end()
    composite_two(qg, vp0)
    arrived("one_ag", some_one)
    source = [rhs[1][p] - buf["w_one"][pl.ds(8 * p, 8)].reshape(128, N) for p in range(2)]

    def listed(p, k):
        return tag_s[k, 0, p]

    def block_at(j):
        return 2 * lax.rem(jnp.int32(j), 8) + (core if j < 8 else 1 - core)

    indices = [[listed(p, block_at(j)) for j in range(16)] for p in range(2)]
    terms = []
    for p in range(2):
        update = product(w1hi[p], w1lo[p], source[p], False)
        terms.extend((indices[p][j], update[8 * j : 8 * j + 8]) for j in range(16))
    nt = buf["nt"]
    for s in range(NR):
        for half in range(2):
            value = None
            for index, piece in terms:
                one = jnp.where(index == 2 * s + half, piece, jnp.zeros((8, N), F32))
                value = one if value is None else value + one
            nt[s, half] = value

    f1a, f1b = buf["a_f1"], buf["b_f1"]
    some_f1 = f1b.at[pl.ds(0, NR - 1)]

    def start_y1():
        exchange_two(vp0, 0)
        arrived("top_rs", some_top)
        start_y1.top = leaf_gather_start("top_ag", 16, total(m_top, NR), buf["w_top"])
        mine = jnp.where(q1 == 0, source[0], source[1])
        f1a[...] = mm("i1", mine, True).reshape(f1a.shape)
        rows_send("f1_rs", lambda peer: f1a.at[peer], f1b.at[row], some_f1)
        f1b[row] = f1a[row]
        arrived("qc", qh)
        composite_two(qh, vp1)

    piece = rows_reduce("nt", nt, buf["mt"], start_y1)
    wt = buf["wt"]
    some = leaf_gather_start("wt", 16, piece, wt, mine8)
    sum_two(0)
    arrived("top_ag", start_y1.top)
    arrived("wt", some)
    owed = jnp.concatenate([wt[:, 0].reshape(128, N), wt[:, 1].reshape(128, N)], axis=0)
    source = rhs[0][...] - (buf["w_top"][...].reshape(256, N) + owed)

    f1y = buf["y_f1"]

    def gather_y1():
        exchange_two(vp0, 1)
        arrived("f1_rs", some_f1)
        f1y[row] = total(f1b, NR)
        gather_y1.some = f1y.at[pl.ds(0, NR - 1)]
        rows_send("f1_ag", lambda peer: f1y.at[row], f1y.at[row], gather_y1.some)

    def solve_y1():
        exchange_two(vp1, 0)
        whi["i2"][...], wlo["i2"][...] = split(w32["i2"][...])
        whi["p3"][...], wlo["p3"][...] = split(w32["p3"][...])
        arrived("f1_ag", gather_y1.some)
        solve_y1.value = mm("i1", rows_value("f1"), False)

    rows_sum("f0", product(i0hi[...], i0lo[...], source, False), gather_y1, solve_y1)
    x0p, x0l, x0r = buf["x0p"], buf["x0l"], buf["x0r"]
    x0p[...] = mm("i0", rows_value("f0"), False).reshape(x0p.shape)
    some = leaf_exchange("x0l", 16, lambda to: x0p.at[:, eighth(to)], x0l, x0p[:, mine8])
    sum_two(1)
    sum_two(2)
    arrived("x0l", some)
    piece = total(x0l, 16)
    rows_gather("x0r", piece, x0r, lambda: exchange_two(vp1, 1))

    def pick_top(index):
        at = jnp.minimum(index, 31)
        held = x0r[lax.div(at, 2), lax.rem(at, 2)]
        return jnp.where(index < 32, held, jnp.zeros((8, N), F32))

    x1p = buf["x1p"]
    for p in range(2):
        chosen = jnp.concatenate([pick_top(indices[p][j]) for j in range(16)], axis=0)
        x1p[p] = -product(w1hi[p], w1lo[p], chosen, True).reshape(8, 16, N)
    x1p[q1] = x1p[q1] + solve_y1.value.reshape(8, 16, N)
    x1l, x1r = buf["x1l"], buf["x1r"]
    some = leaf_exchange("x1l", 16, lambda to: x1p.at[lax.div(to, 8), lax.rem(to, 8)], x1l, x1p[q1, pos[8]])
    piece_top = piece
    x0e, ch2 = buf["x0e"], buf["ch2"]
    remote(x0r, x0e.at[q1], "x0e", {"leaf": lax.rem(leaf + 8, 16)}).start()
    pending.append(("x0e", x0e.at[0]))
    x0e[q1] = x0r[...]

    sum_two(3)
    s30, t30 = buf["s30"], buf["t30"]
    for p in range(8):
        for k in range(2):
            s30[p, k] = pick_top(r3[k, p])
    arrived("x1l", some)
    piece = total(x1l, 16)

    indices_two = [
        [tag_s[k // 2, 0, 2 + 2 * (2 * q1 + p) + k % 2] for k in range(32)] for p in range(2)
    ]

    def fill_t():
        fill_t.out = leaf_gather_start("x0o", 16, piece_top, buf["x0o"], mine8)
        fill_t.three = leaf_exchange("t30", 16, lambda to: s30.at[lax.div(to, 2)], t30, s30[q3], mine8)
        fill_t.own = mm("i2", rows_value("f2"), False)
        arrived("x0e", x0e.at[0])
        for p in range(2):
            for k in range(32):
                at = jnp.minimum(indices_two[p][k], 31)
                for half in range(2):
                    ch2[p, k, pl.ds(8 * half, 8)] = x0e[half, lax.div(at, 2), lax.rem(at, 2)]
        vt[row] = vr[row]
        arrived("vt", vt_all)
        for p in range(2):
            w2hi[p], w2lo[p] = split(vt[:, p].reshape(512, N))

    rows_gather("x1r", piece, x1r, fill_t)

    def pick_one(index):
        held = x1r[jnp.clip(index - 32, 0, 15)]
        mine = jnp.logical_and(index >= 32, index < 48)
        return jnp.where(mine, held, jnp.zeros((16, N), F32))

    x2p, x2l, x2r = buf["x2p"], buf["x2l"], buf["x2r"]
    for p in range(2):
        for k in range(32):
            index = indices_two[p][k]
            ch2[p, k] = jnp.where(index < 32, ch2[p, k], x1r[jnp.clip(index - 32, 0, 15)])
        x2p[p] = -product(w2hi[p], w2lo[p], ch2[p].reshape(512, N), True).reshape(4, 32, N)
    x2p[q2 - 2 * q1] = x2p[q2 - 2 * q1] + fill_t.own.reshape(4, 32, N)
    some = leaf_exchange(
        "x2l", 8, lambda to: x2p.at[lax.div(to, 4), lax.rem(to, 4)], x2l, x2p[q2 - 2 * q1, pos[4]]
    )
    piece_one = piece
    s31, t31 = buf["s31"], buf["t31"]
    for p in range(4):
        for k in range(2):
            s31[p, k] = pick_one(r3[k, 4 * q1 + p])
    arrived("x2l", some)
    piece = total(x2l, 8)

    def fill_o():
        fill_o.three = leaf_exchange("t31", 8, lambda to: s31.at[lax.div(to, 2)], t31, s31[q3 - 4 * q1])
        fill_o.out = leaf_gather_start("x1o", 16, piece_one, buf["x1o"])

    pair_gather("x2r", piece, x2r, fill_o)

    def pick_two(index):
        at = jnp.clip(index - 48, 0, 15)
        held = x2r[lax.div(at, 2), lax.rem(at, 2)]
        return jnp.where(index >= 48, held, jnp.zeros((32, N), F32))

    s32, t32 = buf["s32"], buf["t32"]
    for p in range(2):
        for k in range(2):
            s32[p, k] = pick_two(r3[k, 2 * q2 + p])
    some = leaf_exchange("t32", 4, lambda to: s32.at[lax.div(to, 2)], t32, s32[q3 - 2 * q2])
    piece_two = piece
    arrived("t30", fill_t.three)
    arrived("t31", fill_o.three)
    arrived("t32", some)
    parts = []
    for k in range(2):
        upper = t30[:, k].reshape(128, N) + t31[:, k].reshape(128, N)
        parts.append(upper + t32[:, k].reshape(128, N))

    def last_out():
        last_out.some = leaf_gather_start("x2o", 16, piece_two, buf["x2o"])

    def outputs():
        arrived("x0o", fill_t.out)
        for half in range(2):
            out0[0, pl.ds(128 * half, 128)] = buf["x0o"][:, half].reshape(128, N)
        arrived("x1o", fill_o.out)
        out1[...] = buf["x1o"][...].reshape(out1.shape)
        arrived("x2o", last_out.some)
        out2[...] = buf["x2o"][...].reshape(out2.shape)

    rows_sum("g3", mm("p3", jnp.concatenate(parts, axis=0), False), last_out, outputs)
    x3o = buf["x3o"]
    part = mm("i3", rows_value("f3") - rows_value("g3"), False)
    arrived("x3o", leaf_gather_start("x3o", 16, part, x3o))
    for p in range(8):
        out3[p] = x3o[2 * p] + x3o[2 * p + 1]

    for phase, whole in pending:
        remote(whole, whole, phase, {"rows": lax.rem(row + 1, NR)}).wait_send()


def store(*refs):
    copies = [pltpu.make_async_copy(refs[j], refs[4 + j], refs[8].at[j]) for j in range(4)]
    for copy in copies:
        copy.start()
    for copy in copies:
        copy.wait()


def body(*args):
    vmem = pl.BlockSpec(memory_space=pltpu.VMEM)
    smem = pl.BlockSpec(memory_space=pltpu.SMEM)
    outs = tuple(jax.ShapeDtypeStruct(item.shape, F32) for item in args[:4])
    solved = tuple(
        pl.pallas_call(
            kernel,
            out_shape=outs,
            in_specs=[pl.BlockSpec(memory_space=pltpu.MemorySpace.HBM)] * 11 + [smem] * 3,
            out_specs=[vmem] * 4,
            scratch_shapes=[pltpu.VMEM(BUFS[name], F32) for name in BUF_NAMES]
            + [pltpu.VMEM(shape, BF16) for _, shape in WEIGHTS] * 2
            + [pltpu.VMEM(shape, F32) for _, shape in WEIGHTS]
            + [pltpu.VMEM(shape, F32) for shape in RIGHT]
            + [pltpu.VMEM((2, 128, 128), BF16)] * 2
            + [pltpu.VMEM((2, 512, 128), BF16)] * 2
            + [pltpu.VMEM((256, 512), BF16)] * 4
            + [pltpu.VMEM((512, 128), BF16)] * 2
            + [pltpu.VMEM((256, 256), BF16)] * 2
            + [pltpu.VMEM((NR, 8, N), jnp.int32), pltpu.SMEM((NR, 8, N), jnp.int32)]
            + [pltpu.SemaphoreType.DMA((11,)), pltpu.SemaphoreType.DMA]
            + [pltpu.SemaphoreType.DMA((len(PHASES),)), pltpu.SemaphoreType.DMA((len(PHASES),))],
            compiler_params=pltpu.CompilerParams(
                collective_id=0, has_side_effects=True, vmem_limit_bytes=60 * 1024 * 1024
            ),
        )(*args[:11], *(item.T for item in args[11:]))
    )
    return tuple(
        pl.pallas_call(
            store,
            out_shape=outs,
            in_specs=[vmem] * 4,
            out_specs=[pl.BlockSpec(memory_space=pltpu.MemorySpace.HBM)] * 4,
            scratch_shapes=[pltpu.SemaphoreType.DMA((4,))],
        )(*solved)
    )


def solution(mesh):
    rhs = P(None, "rows", None)
    return jax.shard_map(
        body,
        mesh=mesh,
        in_specs=(rhs,) * 4
        + (P("rows", "leaf"),) * 4
        + (P("leaf", "rows"),) * 3
        + (P(None, "rows"),) * 3,
        out_specs=(rhs,) * 4,
        check_vma=False,
    )
```
